128 devices in a mesh: cluster: 8 (over z, core), seq: 16 (over x, y).
Axes of the slice: x: 4, y: 4, z: 4, core: 2. Of those that a mesh axis runs over, the one named last changes fastest.
Arguments:
- nodes: bfloat16 [65536, 1024], P(('cluster', 'seq')), may hold values from -48 to 48
- w_qkv: bfloat16 [1024, 3072], replicated, may hold values from -0.1875 to 0.1875
- w_out: bfloat16 [1024, 1024], replicated, may hold values from -1.5 to 1.5
- kv_ids: int32 [512, 16], P('cluster'), may hold values from 0 to 511, as said below
- counts: int32 [512], P('cluster'), may hold values from 13 to 16, as said below
Outputs:
- attended_out: bfloat16 [65536, 1024], P(('cluster', 'seq'))
The draws below stay inside these ranges and needn't reach their ends.
Inputs may be any that keep to these rules, and one draw needn't show every extreme that they name: `kv_ids`: entries name blocks; the cluster of block b is b // 64. For query block q, entry 0 is q itself, entries 0 to 11 are distinct blocks of q's cluster, and the last 4 entries are distinct blocks of other clusters. Over all entries of the query blocks of one cluster, at most 16 distinct blocks of any one other cluster are named, and exactly 16 for some pair of clusters. The first counts[q] entries of query block q's list are valid, the others are padding.
All inputs are finite; a program needn't handle non-finite values.
Results may differ from the reference program's by a relative error of at most 0.012.
Values may be sent and summed in bfloat16 or wider, within the bound.
A program may use at most 128 MiB of HBM per device.

```python
import jax
import jax.numpy as jnp
from jax import lax

D = 1024
HEADS = 16
HD = 64
BLK = 128
KVB = 16
REMOTE = 4
QB_CL = 64
REQ = 16
CLUSTERS = 8
QBLOCKS = 512
NODES = 65536


def draw_lists(key):
    qrange = jnp.arange(QBLOCKS, dtype=jnp.int32)
    home = qrange // QB_CL
    inner = qrange % QB_CL
    row_keys = jax.random.split(jax.random.fold_in(key, 101), QBLOCKS)
    shuffled = jax.vmap(lambda k: jax.random.permutation(k, QB_CL - 1))(row_keys).astype(jnp.int32)
    others = (inner[:, None] + 1 + shuffled[:, :KVB - REMOTE - 1]) % QB_CL
    local_part = jnp.concatenate([inner[:, None], others], axis=1) + home[:, None] * QB_CL
    pool_keys = jax.random.split(jax.random.fold_in(key, 102), CLUSTERS * CLUSTERS)
    pools = jax.vmap(lambda k: jax.random.permutation(k, QB_CL))(pool_keys)[:, :REQ].astype(jnp.int32)
    pools = pools.reshape(CLUSTERS, CLUSTERS, REQ)
    offset = jax.random.randint(jax.random.fold_in(key, 103), (QBLOCKS, REMOTE), 1, CLUSTERS).astype(jnp.int32)
    first_off = jnp.where(inner < REQ, 1, offset[:, 0])
    offset = jnp.concatenate([first_off[:, None], offset[:, 1:]], axis=1)
    peer_ids = (home[:, None] + offset) % CLUSTERS
    start = jax.random.randint(jax.random.fold_in(key, 104), (QBLOCKS,), 0, REQ).astype(jnp.int32)
    start = jnp.where(inner < REQ, inner, start)
    pool_pos = (start[:, None] + jnp.arange(REMOTE, dtype=jnp.int32)[None, :]) % REQ
    remote_part = pools[home[:, None], peer_ids, pool_pos] + peer_ids * QB_CL
    lists = jnp.concatenate([local_part, remote_part], axis=1).astype(jnp.int32)
    drawn = jax.random.randint(jax.random.fold_in(key, 105), (QBLOCKS,), KVB - REMOTE + 1, KVB + 1).astype(jnp.int32)
    drawn = jnp.where(inner == 0, KVB, drawn).astype(jnp.int32)
    return (lists, drawn)


def draw_kv_ids(key, part):
    return draw_lists(key)[0]


def draw_counts(key, part):
    return draw_lists(key)[1]


def draw_nodes(key, part):
    values = jnp.clip(jax.random.normal(jax.random.fold_in(key, 7), (NODES, D), jnp.float32), -4.0, 4.0)
    return values.astype(jnp.bfloat16)


def noise(stream_key, dims, spread, most, kind=jnp.bfloat16):
    return jnp.clip(spread * jax.random.normal(stream_key, dims, jnp.float32), -most, most).astype(kind)


def setup_inputs(seed: int = 0) -> dict:
    key_of = jax.random.split(jax.random.key(seed), 6)
    return {
        "nodes": draw_nodes(jax.random.fold_in(key_of[5], 71), 0),
        "w_qkv": noise(key_of[1], (D, 3 * D), D ** -0.5, 0.1875),
        "w_out": noise(key_of[2], (D, D), KVB ** -0.5, 1.5),
        "kv_ids": draw_kv_ids(jax.random.fold_in(key_of[5], 71), 0),
        "counts": draw_counts(jax.random.fold_in(key_of[5], 71), 0),
    }


def reference(nodes, w_qkv, w_out, kv_ids, counts):
    projected = jnp.dot(nodes, w_qkv, preferred_element_type=jnp.float32).astype(jnp.bfloat16)
    blocks = projected.reshape(QBLOCKS, BLK, HEADS, 3, HD)
    queries = blocks[:, :, :, 0]
    keyvals = blocks[:, :, :, 1:]
    groups = QBLOCKS // 4
    slot_ids = jnp.arange(KVB, dtype=jnp.int32)

    def attend(packed):
        query_blk, block_ids, count_blk = packed
        gathered = keyvals[block_ids]
        key_part = gathered[:, :, :, :, 0].astype(jnp.float32)
        value_part = gathered[:, :, :, :, 1].astype(jnp.float32)
        scores = jnp.einsum('qahe,qjkhe->qhajk', query_blk.astype(jnp.float32), key_part) * (HD ** -0.5)
        is_valid = (slot_ids[None, :] < count_blk[:, None])[:, None, None, :, None]
        scores = jnp.where(is_valid, scores, -1e30)
        row_top = jnp.max(scores, axis=(3, 4), keepdims=True)
        exp_scores = jnp.exp(scores - row_top)
        row_total = jnp.sum(exp_scores, axis=(3, 4), keepdims=True)
        weight = (exp_scores / row_total).astype(jnp.bfloat16)
        return jnp.einsum('qhajk,qjkhe->qahe', weight.astype(jnp.float32), value_part).astype(jnp.bfloat16)

    attended = lax.map(attend, (queries.reshape(groups, 4, BLK, HEADS, HD), kv_ids.reshape(groups, 4, KVB), counts.reshape(groups, 4)))
    attended = attended.reshape(QBLOCKS * BLK, HEADS * HD)
    return jnp.dot(attended, w_out, preferred_element_type=jnp.float32).astype(jnp.bfloat16)
```

```python
import functools

import jax
import jax.numpy as jnp
from jax import lax
from jax.experimental import pallas as pl
from jax.experimental.pallas import tpu as pltpu
from jax.sharding import PartitionSpec as P

D = 1024
HEADS = 16
HD = 64
BLK = 128
KVB = 16
REMOTE = 4
NEAR = KVB - REMOTE
QB = 64
REQ = 16
CL = 8
SEQ = 16
OWN = 4
CH = 4
ROWS = BLK // CH
MESH = pl.DeviceIdType.MESH
F32 = jnp.float32
BF16 = jnp.bfloat16


def low_lanes(shape):
    return lax.broadcasted_iota(jnp.int32, shape, len(shape) - 1) < HD


def swap_halves(x):
    return pltpu.roll(x, HD, x.ndim - 1)


def body(
    idx_s,
    cnt_s,
    nodes,
    lists_v,
    w_hbm,
    o_ref,
    w_v,
    kvs,
    kvc0,
    kvc1,
    kvc2,
    kvc3,
    qs,
    qr,
    snd,
    far0,
    far1,
    far2,
    far3,
    lrecv,
    lsm,
    sc,
    acc_v,
    top_v,
    outs,
    ret,
    w_sem,
    l_ss,
    l_rs,
    kv_ss,
    kv_rs,
    q_ss,
    q_rs,
    z_ss,
    z_rs,
    r_ss,
    r_rs,
    own_sem,
    sm_sem,
):
    me = lax.axis_index("seq")
    mc = lax.axis_index("cluster")
    kvc = (kvc0, kvc1, kvc2, kvc3)
    far = (far0, far1, far2, far3)

    barrier = pltpu.get_barrier_semaphore()

    @pl.loop(1, SEQ)
    def _(d):
        pl.semaphore_signal(barrier, inc=1, device_id={"seq": lax.rem(me + d, SEQ)}, device_id_type=MESH)

    @pl.loop(1, CL)
    def _(d):
        pl.semaphore_signal(barrier, inc=1, device_id={"cluster": lax.rem(mc + d, CL)}, device_id_type=MESH)

    def w_copy(g):
        return pltpu.make_async_copy(
            w_hbm.at[:, pl.ds(pl.multiple_of(g * 384, 128), 384)], w_v.at[g], w_sem.at[g]
        )

    @pl.loop(0, 8)
    def _(g):
        w_copy(g).start()

    def project(c, first):
        x = nodes[:, pl.ds(c * ROWS, ROWS), :].reshape(OWN * ROWS, D)

        @pl.loop(0, 8)
        def _(g):
            if first:
                w_copy(g).wait()
            p = jnp.dot(x, w_v[g], preferred_element_type=F32)
            t0, t1, t2 = p[:, :128], p[:, 128:256], p[:, 256:]
            r0, r1 = swap_halves(t0), swap_halves(t1)
            low = low_lanes((OWN * ROWS, 128))
            kv0 = jnp.where(low, r0, r1).astype(BF16)
            kvs[2 * g, c] = kv0.reshape(OWN, ROWS, 128)
            kvs[2 * g + 1, c] = t2.astype(BF16).reshape(OWN, ROWS, 128)
            half = OWN * ROWS // 2
            lowh = low[:half]
            scale = HD**-0.5
            q0 = jnp.where(lowh, t0[:half], r0[half:]) * scale
            q1 = jnp.where(lowh, r1[:half], t1[half:]) * scale
            qs[2 * g, :, pl.ds(c * ROWS, ROWS), :] = q0.astype(BF16).reshape(2, ROWS, 128)
            qs[2 * g + 1, :, pl.ds(c * ROWS, ROWS), :] = q1.astype(BF16).reshape(2, ROWS, 128)

    def kv_copy(c, d):
        peer = lax.rem(me + d, SEQ)
        return pltpu.make_async_remote_copy(
            src_ref=kvs.at[peer, c],
            dst_ref=kvc[c].at[pl.ds(OWN * me, OWN)],
            send_sem=kv_ss.at[c, d],
            recv_sem=kv_rs.at[c, d],
            device_id={"seq": peer},
            device_id_type=MESH,
        )

    def kv_own(c):
        return pltpu.make_async_copy(kvs.at[me, c], kvc[c].at[pl.ds(OWN * me, OWN)], own_sem.at[c])

    def q_copy(i, d):
        peer = lax.rem(me + d, SEQ)
        return pltpu.make_async_remote_copy(
            src_ref=qs.at[peer, i],
            dst_ref=qr.at[i, me],
            send_sem=q_ss.at[i, d],
            recv_sem=q_rs.at[i, d],
            device_id={"seq": peer},
            device_id_type=MESH,
        )

    def q_own(i):
        return pltpu.make_async_copy(qs.at[me, i], qr.at[i, me], own_sem.at[CH + i])

    def list_copy(d):
        peer = lax.rem(mc + d, CL)
        return pltpu.make_async_remote_copy(
            src_ref=lists_v.at[peer],
            dst_ref=lrecv.at[CL - d],
            send_sem=l_ss.at[d],
            recv_sem=l_rs.at[d],
            device_id={"cluster": peer},
            device_id_type=MESH,
        )

    def z_copy(c, d):
        return pltpu.make_async_remote_copy(
            src_ref=snd.at[c, d],
            dst_ref=far[c].at[pl.ds(REQ * mc, REQ)],
            send_sem=z_ss.at[c, d],
            recv_sem=z_rs.at[c, d],
            device_id={"cluster": lax.rem(mc + d, CL)},
            device_id_type=MESH,
        )

    def ret_copy(i, peer, d):
        return pltpu.make_async_remote_copy(
            src_ref=outs.at[i, peer],
            dst_ref=ret.at[i, me],
            send_sem=r_ss.at[i, d],
            recv_sem=r_rs.at[i, d],
            device_id={"seq": peer},
            device_id_type=MESH,
        )

    def ret_own(i):
        return pltpu.make_async_copy(outs.at[i, me], ret.at[i, me], own_sem.at[CH + 2 + i])

    def start_kv(c):
        kv_own(c).start()

        @pl.loop(1, SEQ)
        def _(d):
            kv_copy(c, d).start()

    def start_q(i):
        q_own(i).start()

        @pl.loop(1, SEQ)
        def _(d):
            q_copy(i, d).start()

    def wait_kv(c):
        kv_own(c).wait()

        @pl.loop(1, SEQ)
        def _(d):
            kv_copy(c, d).wait()

    def wait_q(i):
        q_own(i).wait()

        @pl.loop(1, SEQ)
        def _(d):
            q_copy(i, d).wait()

    def pack(c):
        @pl.loop(1, CL)
        def _(d):
            for r in range(REQ):
                snd[c, d, r] = kvc[c][lsm[d, 0, r]]
            z_copy(c, d).start()

    project(0, True)
    pl.semaphore_wait(barrier, SEQ + CL - 2)

    @pl.loop(1, CL)
    def _(d):
        list_copy(d).start()

    start_kv(0)
    project(1, False)
    start_kv(1)
    project(2, False)
    project(3, False)

    @pl.loop(1, CL)
    def _(d):
        list_copy(d).wait()

    sm_copy = pltpu.make_async_copy(lrecv.at[pl.ds(1, CL - 1)], lsm.at[pl.ds(1, CL - 1)], sm_sem)
    sm_copy.start()
    sm_copy.wait()

    wait_kv(0)
    start_kv(2)
    pack(0)
    wait_kv(1)
    start_kv(3)
    pack(1)
    wait_kv(2)
    start_q(0)
    pack(2)
    wait_kv(3)
    start_q(1)
    pack(3)

    def block_of(bufs, b):
        return [bufs[c][b] for c in range(CH)]

    def pair_of(bufs, qb, j):
        return jnp.concatenate(
            block_of(bufs, idx_s[qb * KVB + j]) + block_of(bufs, idx_s[qb * KVB + j + 1]), axis=0
        )

    def score(q, kv):
        return lax.dot_general(q, kv, (((1,), (1,)), ((), ())), preferred_element_type=F32)

    def weigh(s, m, kv):
        p = jnp.exp(s - m).astype(BF16)
        v1 = jnp.where(low_lanes(kv.shape), jnp.ones_like(kv), kv)
        return jnp.dot(p, v1, preferred_element_type=F32)

    def queries(i, s):
        qp = qr[i, s]
        low = low_lanes(qp.shape)
        left = jnp.where(low, qp, jnp.zeros_like(qp))
        right = jnp.where(low, swap_halves(qp.astype(F32)), 0.0).astype(BF16)
        return left, right

    def near(i):
        @pl.loop(0, SEQ)
        def _(s):
            for half, q in enumerate(queries(i, s)):
                qb = s * OWN + i + 2 * half
                top = None
                for jj in range(NEAR // 2):
                    sco = score(q, pair_of(kvc, qb, 2 * jj))
                    sc[half, jj] = sco
                    t = jnp.maximum(sco[:, :BLK], sco[:, BLK:])
                    top = t if top is None else jnp.maximum(top, t)
                m = jnp.max(top, axis=1, keepdims=True)
                acc = None
                for jj in range(NEAR // 2):
                    a = weigh(sc[half, jj], m, pair_of(kvc, qb, 2 * jj))
                    acc = a if acc is None else acc + a
                acc_v[i, s, half] = acc
                top_v[i, s, half] = jnp.broadcast_to(m, (BLK, 128))

    def distant(i):
        @pl.loop(0, SEQ)
        def _(t):
            s = lax.rem(me + t, SEQ)
            packed = []
            for half, q in enumerate(queries(i, s)):
                qb = s * OWN + i + 2 * half
                valid = cnt_s[qb]
                scores, kvs_ = [], []
                mt = top_v[i, s, half]
                m = mt
                for jj in range(REMOTE // 2):
                    kv = pair_of(far, qb, NEAR + 2 * jj)
                    sco = score(q, kv)
                    for part in range(2):
                        piece = sco[:, part * BLK : (part + 1) * BLK]
                        piece = jnp.where(NEAR + 2 * jj + part < valid, piece, -1e30)
                        scores.append(piece)
                        m = jnp.maximum(m, piece)
                    kvs_.append(kv)
                m = jnp.max(m, axis=1, keepdims=True)
                acc = acc_v[i, s, half] * jnp.exp(mt - m)
                for jj in range(REMOTE // 2):
                    both = jnp.concatenate(scores[2 * jj : 2 * jj + 2], axis=1)
                    acc = acc + weigh(both, m, kvs_[jj])
                packed.append(acc)
            low = low_lanes((BLK, 128))
            left, right = packed
            lsw, rsw = swap_halves(left), swap_halves(right)
            value = jnp.where(low, lsw, right)
            total = jnp.where(low, left, rsw)
            outs[i, s] = (value / total).astype(BF16)

            @pl.when(t > 0)
            def _():
                ret_copy(i, s, t).start()

    wait_q(0)
    near(0)
    wait_q(1)
    near(1)

    for c in range(CH):

        @pl.loop(1, CL)
        def _(d, c=c):
            z_copy(c, d).wait()

    for i in range(2):
        distant(i)
        ret_own(i).start()

    for i in range(2):
        ret_own(i).wait()

        @pl.loop(1, SEQ)
        def _(d, i=i):
            ret_copy(i, lax.rem(me + d, SEQ), d).wait()

    for g in range(HEADS // 2):
        for i in range(2):
            a = ret[i, 2 * g].astype(F32)
            b = ret[i, 2 * g + 1].astype(F32)
            low = low_lanes(a.shape)
            o_ref[i, :, g * 128 : (g + 1) * 128] = jnp.where(low, a, swap_halves(b)).astype(BF16)
            o_ref[2 + i, :, g * 128 : (g + 1) * 128] = jnp.where(low, swap_halves(a), b).astype(BF16)


def request_lists(kv_ids, cluster):
    named = kv_ids[:, NEAR:]
    blocks = jnp.arange(CL * QB, dtype=jnp.int32)
    onehot = named.reshape(-1, 1) == blocks[None, :]
    present = jnp.any(onehot, axis=0).reshape(CL, QB)
    inner = jnp.arange(QB, dtype=jnp.int32)
    rank = jnp.sum(
        jnp.where(present[:, None, :] & (inner[None, None, :] < inner[None, :, None]), 1, 0), axis=2
    )
    slot = jnp.arange(REQ, dtype=jnp.int32)
    hit = present[:, None, :] & (rank[:, None, :] == slot[None, :, None])
    lists = jnp.sum(jnp.where(hit, inner[None, None, :], 0), axis=2)
    place = (rank + REQ * jnp.arange(CL, dtype=jnp.int32)[:, None]).reshape(-1)
    far = jnp.sum(jnp.where(onehot, place[None, :], 0), axis=1).reshape(QB, REMOTE)
    idx = jnp.concatenate([kv_ids[:, :NEAR] - cluster * QB, far], axis=1).reshape(-1)
    lists = jnp.broadcast_to(jnp.pad(lists, ((0, 0), (0, 128 - REQ)))[:, None, :], (CL, 8, 128))
    return idx, lists


def on_device(nodes, w_qkv, w_out, kv_ids, counts):
    idx, lists = request_lists(kv_ids, lax.axis_index("cluster"))
    vm = pl.BlockSpec(memory_space=pltpu.VMEM)
    sm = pl.BlockSpec(memory_space=pltpu.SMEM)
    dma = pltpu.SemaphoreType.DMA
    attended = pl.pallas_call(
        body,
        out_shape=jax.ShapeDtypeStruct((OWN, BLK, D), BF16),
        in_specs=[sm, sm, vm, vm, pl.BlockSpec(memory_space=pl.ANY)],
        out_specs=vm,
        scratch_shapes=[
            pltpu.VMEM((8, D, 384), BF16),
            pltpu.VMEM((HEADS, CH, OWN, ROWS, 128), BF16),
            *[pltpu.VMEM((QB, ROWS, 128), BF16) for _ in range(CH)],
            pltpu.VMEM((HEADS, 2, BLK, 128), BF16),
            pltpu.VMEM((2, SEQ, BLK, 128), BF16),
            pltpu.VMEM((CH, CL, REQ, ROWS, 128), BF16),
            *[pltpu.VMEM((CL * REQ, ROWS, 128), BF16) for _ in range(CH)],
            pltpu.VMEM((CL, 8, 128), jnp.int32),
            pltpu.SMEM((CL, 8, 128), jnp.int32),
            pltpu.VMEM((2, NEAR // 2, BLK, 2 * BLK), F32),
            pltpu.VMEM((2, SEQ, 2, BLK, 128), F32),
            pltpu.VMEM((2, SEQ, 2, BLK, 128), F32),
            pltpu.VMEM((2, SEQ, BLK, 128), BF16),
            pltpu.VMEM((2, SEQ, BLK, 128), BF16),
            dma((8,)),
            dma((CL,)),
            dma((CL,)),
            dma((CH, SEQ)),
            dma((CH, SEQ)),
            dma((2, SEQ)),
            dma((2, SEQ)),
            dma((CH, CL)),
            dma((CH, CL)),
            dma((2, SEQ)),
            dma((2, SEQ)),
            dma((CH + 4,)),
            dma(()),
        ],
        compiler_params=pltpu.CompilerParams(
            collective_id=0, has_side_effects=True, vmem_limit_bytes=60 << 20
        ),
        name="sublayer",
    )(idx, counts, nodes.reshape(OWN, BLK, D), lists, w_qkv)
    return jnp.dot(attended.reshape(OWN * BLK, D), w_out, preferred_element_type=F32).astype(BF16)


def solution(mesh):
    placed = (P(("cluster", "seq"), None), P(), P(), P("cluster", None), P("cluster"))
    return jax.shard_map(
        on_device,
        mesh=mesh,
        in_specs=placed,
        out_specs=P(("cluster", "seq"), None),
        check_vma=False,
    )
```

```python
import functools

import jax
import jax.numpy as jnp
from jax import lax
from jax.experimental import pallas as pl
from jax.experimental.pallas import tpu as pltpu
from jax.sharding import PartitionSpec as P

D = 1024
HEADS = 16
HD = 64
BLK = 128
KVB = 16
REMOTE = 4
NEAR = KVB - REMOTE
QB = 64
REQ = 16
CL = 8
SEQ = 16
OWN = 4
CH = 4
ROWS = BLK // CH
GROUPS = 4
WCOL = 3 * D // GROUPS
SIDE = 8
MESH = pl.DeviceIdType.MESH
F32 = jnp.float32
BF16 = jnp.bfloat16


def low_lanes(shape):
    return lax.broadcasted_iota(jnp.int32, shape, len(shape) - 1) < HD


def swap_halves(x):
    return pltpu.roll(x, HD, x.ndim - 1)


def body(
    ids_s,
    cnt_s,
    nodes,
    ids_v,
    w_hbm,
    o_ref,
    w_v,
    kvs,
    kvc0,
    kvc1,
    kvc2,
    kvc3,
    qs,
    qr,
    snd,
    far0,
    far1,
    far2,
    far3,
    lsend,
    lrecv,
    lsm,
    far_v,
    far_s,
    sc,
    acc_v,
    top_v,
    outs,
    ret,
    w_sem,
    l_ss,
    l_rs,
    kv_ss,
    kv_rs,
    q_ss,
    q_rs,
    z_ss,
    z_rs,
    r_ss,
    r_rs,
    own_sem,
    sm_sem,
):
    me = lax.axis_index("seq")
    mc = lax.axis_index("cluster")
    kvc = (kvc0, kvc1, kvc2, kvc3)
    far = (far0, far1, far2, far3)

    barrier = pltpu.get_barrier_semaphore()

    @pl.loop(1, SEQ)
    def _(d):
        pl.semaphore_signal(barrier, inc=1, device_id={"seq": lax.rem(me + d, SEQ)}, device_id_type=MESH)

    @pl.loop(1, CL)
    def _(d):
        pl.semaphore_signal(barrier, inc=1, device_id={"cluster": lax.rem(mc + d, CL)}, device_id_type=MESH)

    def w_copy(g):
        return pltpu.make_async_copy(
            w_hbm.at[:, pl.ds(pl.multiple_of(g * WCOL, 128), WCOL)], w_v.at[g], w_sem.at[g]
        )

    @pl.loop(0, GROUPS)
    def _(g):
        w_copy(g).start()

    @pl.loop(0, GROUPS)
    def _(g):
        w_copy(g).wait()
        p = jnp.dot(nodes[...], w_v[g], preferred_element_type=F32)
        low = low_lanes((OWN * BLK, 128))
        half = OWN * BLK // 2
        scale = HD**-0.5
        for k in range(2):
            t0, t1, t2 = (p[:, 384 * k + 128 * n : 384 * k + 128 * n + 128] for n in range(3))
            r0, r1 = swap_halves(t0), swap_halves(t1)
            h0 = 4 * g + 2 * k
            kv0 = jnp.where(low, r0, r1).astype(BF16).reshape(OWN, BLK, 128)
            kv1 = t2.astype(BF16).reshape(OWN, BLK, 128)
            for c in range(CH):
                kvs[h0, c] = kv0[:, c * ROWS : (c + 1) * ROWS]
                kvs[h0 + 1, c] = kv1[:, c * ROWS : (c + 1) * ROWS]
            q0 = jnp.where(low[:half], t0[:half], r0[half:]) * scale
            q1 = jnp.where(low[:half], r1[:half], t1[half:]) * scale
            qs[h0] = q0.astype(BF16).reshape(2, BLK, 128)
            qs[h0 + 1] = q1.astype(BF16).reshape(2, BLK, 128)

    def kv_copy(c, d):
        peer = lax.rem(me + d, SEQ)
        return pltpu.make_async_remote_copy(
            src_ref=kvs.at[peer, c],
            dst_ref=kvc[c].at[pl.ds(OWN * me, OWN)],
            send_sem=kv_ss.at[c, d],
            recv_sem=kv_rs.at[c, d],
            device_id={"seq": peer},
            device_id_type=MESH,
        )

    def kv_own(c):
        return pltpu.make_async_copy(kvs.at[me, c], kvc[c].at[pl.ds(OWN * me, OWN)], own_sem.at[c])

    def q_copy(i, d):
        peer = lax.rem(me + d, SEQ)
        return pltpu.make_async_remote_copy(
            src_ref=qs.at[peer, i],
            dst_ref=qr.at[i, me],
            send_sem=q_ss.at[i, d],
            recv_sem=q_rs.at[i, d],
            device_id={"seq": peer},
            device_id_type=MESH,
        )

    def q_own(i):
        return pltpu.make_async_copy(qs.at[me, i], qr.at[i, me], own_sem.at[CH + i])

    def list_copy(d):
        peer = lax.rem(mc + d, CL)
        return pltpu.make_async_remote_copy(
            src_ref=lsend.at[peer],
            dst_ref=lrecv.at[CL - d],
            send_sem=l_ss.at[d],
            recv_sem=l_rs.at[d],
            device_id={"cluster": peer},
            device_id_type=MESH,
        )

    def z_copy(c, d):
        return pltpu.make_async_remote_copy(
            src_ref=snd.at[c, d],
            dst_ref=far[c].at[pl.ds(REQ * mc, REQ)],
            send_sem=z_ss.at[c, d],
            recv_sem=z_rs.at[c, d],
            device_id={"cluster": lax.rem(mc + d, CL)},
            device_id_type=MESH,
        )

    def ret_copy(i, peer, d):
        return pltpu.make_async_remote_copy(
            src_ref=outs.at[i, peer],
            dst_ref=ret.at[i, me],
            send_sem=r_ss.at[i, d],
            recv_sem=r_rs.at[i, d],
            device_id={"seq": peer},
            device_id_type=MESH,
        )

    def ret_own(i):
        return pltpu.make_async_copy(outs.at[i, me], ret.at[i, me], own_sem.at[CH + 2 + i])

    def start(own, copy):
        own.start()

        @pl.loop(1, SEQ)
        def _(d):
            copy(d).start()

    def start_after(done, own, copy):
        own.start()

        @pl.loop(1, SEQ)
        def _(d):
            done(d).wait_send()
            copy(d).start()

    def landed(own, copy):
        own.wait()

        @pl.loop(1, SEQ)
        def _(d):
            copy(d).wait_recv()

    def kv(c):
        return functools.partial(kv_copy, c)

    def qq(i):
        return functools.partial(q_copy, i)

    def pack(c):
        @pl.loop(1, CL)
        def _(d):
            for r in range(REQ):
                snd[c, d, r] = kvc[c][lsm[d, r, 0] & (QB - 1)]
            z_copy(c, d).start()

    pl.semaphore_wait(barrier, SEQ + CL - 2)
    start(kv_own(0), kv(0))

    lane = lax.broadcasted_iota(jnp.int32, (QB, CL * QB), 1)
    hits = [ids_v[:, NEAR + j : NEAR + j + 1] == lane for j in range(REMOTE)]
    named = jnp.where(hits[0] | hits[1] | hits[2] | hits[3], 1.0, 0.0)
    present = jnp.max(named, axis=0, keepdims=True)
    present = jnp.broadcast_to(present, (8, CL * QB))
    lane8 = lax.broadcasted_iota(jnp.int32, (8, CL * QB), 1)
    inner = lane8 % QB
    rank = present
    step = 1
    while step < QB:
        rank = rank + jnp.where(inner >= step, pltpu.roll(rank, step, 1), 0.0)
        step *= 2
    rank = rank - present
    place = rank + (lane8 // QB * REQ).astype(F32)
    for j in range(REMOTE):
        at = jnp.sum(jnp.where(hits[j], place[:1], 0.0), axis=1, keepdims=True)
        far_v[j] = jnp.broadcast_to(at, (QB, 128)).astype(jnp.int32)
    slot = lax.broadcasted_iota(jnp.int32, (REQ, CL * QB), 0).astype(F32)
    wanted = jnp.where((slot == rank[:1]) & (present[:1] > 0.5), inner[:1].astype(F32), 0.0)
    lane_r = lax.broadcasted_iota(jnp.int32, (REQ, 128), 1)
    for p in range(CL):
        tile = wanted[:, p // 2 * 128 : p // 2 * 128 + 128]
        mine = jnp.where((lane_r >= HD) == (p % 2 == 1), tile, 0.0)
        block = jnp.sum(mine, axis=1, keepdims=True)
        lsend[p] = jnp.broadcast_to(block, (REQ, 128)).astype(jnp.int32)

    @pl.loop(1, CL)
    def _(d):
        list_copy(d).start()

    far_copy = pltpu.make_async_copy(far_v, far_s, sm_sem.at[1])
    far_copy.start()

    start_after(kv(0), kv_own(1), kv(1))

    @pl.loop(1, CL)
    def _(d):
        list_copy(d).wait()

    sm_copy = pltpu.make_async_copy(
        lrecv.at[pl.ds(1, CL - 1)], lsm.at[pl.ds(1, CL - 1)], sm_sem.at[0]
    )
    sm_copy.start()
    sm_copy.wait()
    far_copy.wait()

    landed(kv_own(0), kv(0))
    pack(0)
    start_after(kv(1), kv_own(2), kv(2))
    landed(kv_own(1), kv(1))
    pack(1)
    start_after(kv(2), kv_own(3), kv(3))
    landed(kv_own(2), kv(2))
    pack(2)
    start_after(kv(3), q_own(0), qq(0))
    landed(kv_own(3), kv(3))
    pack(3)
    start_after(qq(0), q_own(1), qq(1))

    def block_of(bufs, b):
        return [bufs[c][b] for c in range(CH)]

    def pair_of(bufs, b0, b1):
        return jnp.concatenate(block_of(bufs, b0) + block_of(bufs, b1), axis=0)

    def near_pair(qb, j):
        return pair_of(kvc, ids_s[qb, j] & (QB - 1), ids_s[qb, j + 1] & (QB - 1))

    def far_pair(qb, j):
        last = CL * REQ - 1
        return pair_of(far, far_s[j, qb, 0] & last, far_s[j + 1, qb, 0] & last)

    def score(q, kv):
        return lax.dot_general(q, kv, (((1,), (1,)), ((), ())), preferred_element_type=F32)

    def weigh(s, m, kv):
        p = jnp.exp(s - m).astype(BF16)
        v1 = jnp.where(low_lanes(kv.shape), jnp.ones_like(kv), kv)
        return jnp.dot(p, v1, preferred_element_type=F32)

    def queries(i, s):
        qp = qr[i, s]
        low = low_lanes(qp.shape)
        left = jnp.where(low, qp, jnp.zeros_like(qp))
        right = jnp.where(low, swap_halves(qp.astype(F32)), 0.0).astype(BF16)
        return left, right

    def items_of(i, first):
        items = []
        for u in range(SIDE // 2):
            s = lax.rem(me + first + u, SEQ)
            for half, q in enumerate(queries(i, s)):
                items.append((s, half, q, s * OWN + i + 2 * half))
        return items

    def near(i):
        @pl.loop(0, 2 * SEQ // SIDE)
        def _(t):
            items = items_of(i, t * (SIDE // 2))
            tops = [None] * SIDE
            for jj in range(NEAR // 2):
                for g, (s, half, q, qb) in enumerate(items):
                    sco = score(q, near_pair(qb, 2 * jj))
                    sc[g, jj] = sco
                    top = jnp.maximum(sco[:, :BLK], sco[:, BLK:])
                    tops[g] = top if jj == 0 else jnp.maximum(tops[g], top)
            tops = [jnp.max(top, axis=1, keepdims=True) for top in tops]
            accs = [None] * SIDE
            for jj in range(NEAR // 2):
                for g, (s, half, q, qb) in enumerate(items):
                    a = weigh(sc[g, jj], tops[g], near_pair(qb, 2 * jj))
                    accs[g] = a if jj == 0 else accs[g] + a
            for g, (s, half, q, qb) in enumerate(items):
                acc_v[i, s, half] = accs[g]
                top_v[i, s, half] = jnp.broadcast_to(tops[g], (BLK, 128))

    def distant(i):
        @pl.loop(0, 2 * SEQ // SIDE)
        def _(t):
            items = items_of(i, t * (SIDE // 2))
            pairs = [[far_pair(qb, 2 * jj) for jj in range(REMOTE // 2)] for _, _, _, qb in items]
            scores, tops, accs = [], [], []
            for g, (s, half, q, qb) in enumerate(items):
                pieces = []
                for jj in range(REMOTE // 2):
                    sco = score(q, pairs[g][jj])
                    for part in range(2):
                        piece = sco[:, part * BLK : (part + 1) * BLK]
                        valid = NEAR + 2 * jj + part < cnt_s[qb]
                        pieces.append(jnp.where(valid, piece, -1e30))
                scores.append(pieces)
            for g, (s, half, q, qb) in enumerate(items):
                m = top_v[i, s, half]
                for piece in scores[g]:
                    m = jnp.maximum(m, piece)
                tops.append(jnp.max(m, axis=1, keepdims=True))
            for g, (s, half, q, qb) in enumerate(items):
                acc = acc_v[i, s, half] * jnp.exp(top_v[i, s, half] - tops[g])
                for jj in range(REMOTE // 2):
                    both = jnp.concatenate(scores[g][2 * jj : 2 * jj + 2], axis=1)
                    acc = acc + weigh(both, tops[g], pairs[g][jj])
                accs.append(acc)
            low = low_lanes((BLK, 128))
            for u in range(SIDE // 2):
                s = items[2 * u][0]
                left, right = accs[2 * u : 2 * u + 2]
                lsw, rsw = swap_halves(left), swap_halves(right)
                value = jnp.where(low, lsw, right)
                total = jnp.where(low, left, rsw)
                outs[i, s] = (value / total).astype(BF16)

            for u in range(SIDE // 2):
                d = t * (SIDE // 2) + u

                @pl.when(d > 0)
                def _(d=d):
                    ret_copy(i, lax.rem(me + d, SEQ), d).start()

    landed(q_own(0), qq(0))
    near(0)
    landed(q_own(1), qq(1))
    near(1)

    for c in range(CH):

        @pl.loop(1, CL)
        def _(d, c=c):
            z_copy(c, d).wait()

    for i in range(2):
        distant(i)
        ret_own(i).start()

    @pl.loop(1, SEQ)
    def _(d):
        q_copy(1, d).wait_send()

    for i in range(2):
        ret_own(i).wait()

        @pl.loop(1, SEQ)
        def _(d, i=i):
            ret_copy(i, lax.rem(me + d, SEQ), d).wait()

    for g in range(HEADS // 2):
        for i in range(2):
            a = ret[i, 2 * g].astype(F32)
            b = ret[i, 2 * g + 1].astype(F32)
            low = low_lanes(a.shape)
            o_ref[i, :, g * 128 : (g + 1) * 128] = jnp.where(low, a, swap_halves(b)).astype(BF16)
            o_ref[2 + i, :, g * 128 : (g + 1) * 128] = jnp.where(low, swap_halves(a), b).astype(BF16)


def on_device(nodes, w_qkv, w_out, kv_ids, counts):
    vm = pl.BlockSpec(memory_space=pltpu.VMEM)
    sm = pl.BlockSpec(memory_space=pltpu.SMEM)
    dma = pltpu.SemaphoreType.DMA
    attended = pl.pallas_call(
        body,
        out_shape=jax.ShapeDtypeStruct((OWN, BLK, D), BF16),
        in_specs=[sm, sm, vm, vm, pl.BlockSpec(memory_space=pl.ANY)],
        out_specs=vm,
        scratch_shapes=[
            pltpu.VMEM((GROUPS, D, WCOL), BF16),
            pltpu.VMEM((HEADS, CH, OWN, ROWS, 128), BF16),
            *[pltpu.VMEM((QB, ROWS, 128), BF16) for _ in range(CH)],
            pltpu.VMEM((HEADS, 2, BLK, 128), BF16),
            pltpu.VMEM((2, SEQ, BLK, 128), BF16),
            pltpu.VMEM((CH, CL, REQ, ROWS, 128), BF16),
            *[pltpu.VMEM((CL * REQ, ROWS, 128), BF16) for _ in range(CH)],
            pltpu.VMEM((CL, REQ, 128), jnp.int32),
            pltpu.VMEM((CL, REQ, 128), jnp.int32),
            pltpu.SMEM((CL, REQ, 128), jnp.int32),
            pltpu.VMEM((REMOTE, QB, 128), jnp.int32),
            pltpu.SMEM((REMOTE, QB, 128), jnp.int32),
            pltpu.VMEM((SIDE, NEAR // 2, BLK, 2 * BLK), F32),
            pltpu.VMEM((2, SEQ, 2, BLK, 128), F32),
            pltpu.VMEM((2, SEQ, 2, BLK, 128), F32),
            pltpu.VMEM((2, SEQ, BLK, 128), BF16),
            pltpu.VMEM((2, SEQ, BLK, 128), BF16),
            dma((GROUPS,)),
            dma((CL,)),
            dma((CL,)),
            dma((CH, SEQ)),
            dma((CH, SEQ)),
            dma((2, SEQ)),
            dma((2, SEQ)),
            dma((CH, CL)),
            dma((CH, CL)),
            dma((2, SEQ)),
            dma((2, SEQ)),
            dma((CH + 4,)),
            dma((2,)),
        ],
        compiler_params=pltpu.CompilerParams(
            collective_id=0, has_side_effects=True, vmem_limit_bytes=60 << 20
        ),
        name="sublayer",
    )(kv_ids, counts, nodes, kv_ids, w_qkv)
    return jnp.dot(attended.reshape(OWN * BLK, D), w_out, preferred_element_type=F32).astype(BF16)


def solution(mesh):
    placed = (P(("cluster", "seq"), None), P(), P(), P("cluster", None), P("cluster"))
    return jax.shard_map(
        on_device,
        mesh=mesh,
        in_specs=placed,
        out_specs=P(("cluster", "seq"), None),
        check_vma=False,
    )
```

```python
import functools

import jax
import jax.numpy as jnp
from jax import lax
from jax.experimental import pallas as pl
from jax.experimental.pallas import tpu as pltpu
from jax.sharding import PartitionSpec as P

D = 1024
HEADS = 16
HD = 64
BLK = 128
KVB = 16
REMOTE = 4
NEAR = KVB - REMOTE
QB = 64
REQ = 16
CL = 8
SEQ = 16
OWN = 4
ROWS = (16, 16, 32, 32, 32)
CH = len(ROWS)
FIRST = tuple(sum(ROWS[:c]) for c in range(CH))
GROUPS = 4
WCOL = 3 * D // GROUPS
SIDE = 8
MESH = pl.DeviceIdType.MESH
F32 = jnp.float32
BF16 = jnp.bfloat16


def low_lanes(shape):
    return lax.broadcasted_iota(jnp.int32, shape, len(shape) - 1) < HD


def swap_halves(x):
    return pltpu.roll(x, HD, x.ndim - 1)


def body(ids_s, cnt_s, nodes, ids_v, w_hbm, wo_hbm, o_ref, *scratch):
    me = lax.axis_index("seq")
    mc = lax.axis_index("cluster")
    scratch = list(scratch)

    def take(n):
        got = scratch[:n]
        del scratch[:n]
        return got

    kvs, kvc, snd, far = take(CH), take(CH), take(CH), take(CH)
    w_v, wo_v, qs, qr, lsend, lrecv, lsm, far_v, far_s, sc, acc_v, top_v, outs, ret, att = take(15)
    w_sem, l_ss, l_rs, kv_ss, kv_rs, q_ss, q_rs, z_ss, z_rs, r_ss, r_rs, own_sem, sm_sem = scratch

    barrier = pltpu.get_barrier_semaphore()

    @pl.loop(1, SEQ)
    def _(d):
        pl.semaphore_signal(barrier, inc=1, device_id={"seq": lax.rem(me + d, SEQ)}, device_id_type=MESH)

    @pl.loop(1, CL)
    def _(d):
        pl.semaphore_signal(barrier, inc=1, device_id={"cluster": lax.rem(mc + d, CL)}, device_id_type=MESH)

    def w_copy(k):
        g = lax.rem(me // GROUPS + k, GROUPS)
        return pltpu.make_async_copy(
            w_hbm.at[:, pl.ds(pl.multiple_of(g * WCOL, 128), WCOL)], w_v.at[k], w_sem.at[k]
        )

    @pl.loop(0, GROUPS)
    def _(k):
        w_copy(k).start()

    wo_copy = pltpu.make_async_copy(wo_hbm, wo_v, w_sem.at[GROUPS])
    wo_copy.start()

    def kv_copy(c, d):
        peer = lax.rem(me + d, SEQ)
        return pltpu.make_async_remote_copy(
            src_ref=kvs[c].at[peer],
            dst_ref=kvc[c].at[pl.ds(OWN * me, OWN)],
            send_sem=kv_ss.at[c, d],
            recv_sem=kv_rs.at[c, d],
            device_id={"seq": peer},
            device_id_type=MESH,
        )

    def kv_own(c):
        return pltpu.make_async_copy(kvs[c].at[me], kvc[c].at[pl.ds(OWN * me, OWN)], own_sem.at[c])

    def q_copy(i, d):
        peer = lax.rem(me + d, SEQ)
        return pltpu.make_async_remote_copy(
            src_ref=qs.at[peer, i],
            dst_ref=qr.at[i, me],
            send_sem=q_ss.at[i, d],
            recv_sem=q_rs.at[i, d],
            device_id={"seq": peer},
            device_id_type=MESH,
        )

    def q_own(i):
        return pltpu.make_async_copy(qs.at[me, i], qr.at[i, me], own_sem.at[CH + i])

    def list_copy(d):
        peer = lax.rem(mc + d, CL)
        return pltpu.make_async_remote_copy(
            src_ref=lsend.at[peer],
            dst_ref=lrecv.at[CL - d],
            send_sem=l_ss.at[d],
            recv_sem=l_rs.at[d],
            device_id={"cluster": peer},
            device_id_type=MESH,
        )

    def z_copy(c, d):
        return pltpu.make_async_remote_copy(
            src_ref=snd[c].at[d],
            dst_ref=far[c].at[pl.ds(REQ * mc, REQ)],
            send_sem=z_ss.at[c, d],
            recv_sem=z_rs.at[c, d],
            device_id={"cluster": lax.rem(mc + d, CL)},
            device_id_type=MESH,
        )

    def ret_copy(i, peer, d):
        return pltpu.make_async_remote_copy(
            src_ref=outs.at[i, peer],
            dst_ref=ret.at[i, me],
            send_sem=r_ss.at[i, d],
            recv_sem=r_rs.at[i, d],
            device_id={"seq": peer},
            device_id_type=MESH,
        )

    def ret_own(i):
        return pltpu.make_async_copy(outs.at[i, me], ret.at[i, me], own_sem.at[CH + 2 + i])

    def start(own, copy):
        own.start()

        @pl.loop(1, SEQ)
        def _(d):
            copy(d).start()

    def start_after(done, own, copy):
        own.start()

        @pl.loop(1, SEQ)
        def _(d):
            done(d).wait_send()
            copy(d).start()

    def landed(own, copy):
        own.wait()

        @pl.loop(1, SEQ)
        def _(d):
            copy(d).wait_recv()

    def kv(c):
        return functools.partial(kv_copy, c)

    def qq(i):
        return functools.partial(q_copy, i)

    def pack(c):
        @pl.loop(1, CL)
        def _(d):
            for r in range(REQ):
                snd[c][d, r] = kvc[c][lsm[d, 0, r] & (QB - 1)]
            z_copy(c, d).start()

    lane = lax.broadcasted_iota(jnp.int32, (QB, CL * QB), 1)
    hits = [ids_v[:, NEAR + j : NEAR + j + 1] == lane for j in range(REMOTE)]
    named = jnp.where(hits[0] | hits[1] | hits[2] | hits[3], 1.0, 0.0)
    present = jnp.max(named, axis=0, keepdims=True)
    present = jnp.broadcast_to(present, (8, CL * QB))
    lane8 = lax.broadcasted_iota(jnp.int32, (8, CL * QB), 1)
    inner = lane8 % QB
    rank = present
    step = 1
    while step < QB:
        rank = rank + jnp.where(inner >= step, pltpu.roll(rank, step, 1), 0.0)
        step *= 2
    rank = rank - present
    slot = lax.broadcasted_iota(jnp.int32, (REQ, CL * QB), 0).astype(F32)
    wanted = jnp.where((slot == rank[:1]) & (present[:1] > 0.5), 1.0, 0.0).astype(BF16)
    sub8 = lax.broadcasted_iota(jnp.int32, (CL, CL * QB), 0)
    worth = jnp.where(lane8 // QB == sub8, inner, 0).astype(F32).astype(BF16)
    wanted = jnp.concatenate([wanted, jnp.zeros((128 - REQ, CL * QB), BF16)], axis=0)
    lists = lax.dot_general(
        worth, wanted, (((1,), (1,)), ((), ())), preferred_element_type=F32
    ).astype(jnp.int32)
    for p in range(CL):
        lsend[p] = lists[p : p + 1]
    place = rank + (lane8 // QB * REQ).astype(F32)
    lane_q = lax.broadcasted_iota(jnp.int32, (QB, 128), 1)
    table = jnp.zeros((QB, 128), F32)
    for j in range(REMOTE):
        at = jnp.sum(jnp.where(hits[j], place[:1], 0.0), axis=1, keepdims=True)
        table = jnp.where(lane_q == j, at, table)
    far_v[...] = table.astype(jnp.int32)
    far_copy = pltpu.make_async_copy(far_v, far_s, sm_sem.at[1])
    far_copy.start()

    @pl.loop(0, GROUPS)
    def _(k):
        g = lax.rem(me // GROUPS + k, GROUPS)
        w_copy(k).wait()
        p = jnp.dot(nodes[...], w_v[k], preferred_element_type=F32)
        low = low_lanes((OWN * BLK, 128))
        half = OWN * BLK // 2
        scale = HD**-0.5
        for n in range(2):
            t0, t1, t2 = (p[:, 384 * n + 128 * e : 384 * n + 128 * e + 128] for e in range(3))
            r0, r1 = swap_halves(t0), swap_halves(t1)
            h0 = 4 * g + 2 * n
            kv0 = jnp.where(low, r0, r1).astype(BF16).reshape(OWN, BLK, 128)
            kv1 = t2.astype(BF16).reshape(OWN, BLK, 128)
            for c in range(CH):
                kvs[c][h0] = kv0[:, FIRST[c] : FIRST[c] + ROWS[c]]
                kvs[c][h0 + 1] = kv1[:, FIRST[c] : FIRST[c] + ROWS[c]]
            q0 = jnp.where(low[:half], t0[:half], r0[half:]) * scale
            q1 = jnp.where(low[:half], r1[:half], t1[half:]) * scale
            qs[h0] = q0.astype(BF16).reshape(2, BLK, 128)
            qs[h0 + 1] = q1.astype(BF16).reshape(2, BLK, 128)

        @pl.when(k == 0)
        def _():
            pl.semaphore_wait(barrier, SEQ + CL - 2)

            @pl.loop(1, CL)
            def _(d):
                list_copy(d).start()

        @pl.loop(0, HEADS // GROUPS)
        def _(h):
            d = lax.rem(g * (HEADS // GROUPS) + h + SEQ - me, SEQ)

            @pl.when(d > 0)
            def _():
                kv_copy(0, d).start()

    kv_own(0).start()
    start_after(kv(0), kv_own(1), kv(1))

    @pl.loop(1, CL)
    def _(d):
        list_copy(d).wait()

    sm_copy = pltpu.make_async_copy(
        lrecv.at[pl.ds(1, CL - 1)], lsm.at[pl.ds(1, CL - 1)], sm_sem.at[0]
    )
    sm_copy.start()
    sm_copy.wait()

    for c in range(CH):
        landed(kv_own(c), kv(c))
        pack(c)
        if c + 2 < CH:
            start_after(kv(c + 1), kv_own(c + 2), kv(c + 2))
        elif c + 2 == CH:
            start_after(kv(c + 1), q_own(0), qq(0))
    start_after(qq(0), q_own(1), qq(1))

    def block_of(bufs, b):
        return [bufs[c][b] for c in range(CH)]

    def pair_of(bufs, b0, b1):
        return jnp.concatenate(block_of(bufs, b0) + block_of(bufs, b1), axis=0)

    def near_pair(qb, j):
        return pair_of(kvc, ids_s[qb, j] & (QB - 1), ids_s[qb, j + 1] & (QB - 1))

    def far_pair(qb, j):
        last = CL * REQ - 1
        return pair_of(far, far_s[qb, j] & last, far_s[qb, j + 1] & last)

    def score(q, kv):
        return lax.dot_general(q, kv, (((1,), (1,)), ((), ())), preferred_element_type=F32)

    def weigh(s, m, kv):
        p = jnp.exp(s - m).astype(BF16)
        v1 = jnp.where(low_lanes(kv.shape), jnp.ones_like(kv), kv)
        return jnp.dot(p, v1, preferred_element_type=F32)

    def queries(i, s):
        qp = qr[i, s]
        low = low_lanes(qp.shape)
        left = jnp.where(low, qp, jnp.zeros_like(qp))
        right = jnp.where(low, swap_halves(qp.astype(F32)), 0.0).astype(BF16)
        return left, right

    def items_of(i, first):
        items = []
        for u in range(SIDE // 2):
            s = lax.rem(me + first + u, SEQ)
            for half, q in enumerate(queries(i, s)):
                items.append((s, half, q, s * OWN + i + 2 * half))
        return items

    def near(i):
        @pl.loop(0, 2 * SEQ // SIDE)
        def _(t):
            items = items_of(i, t * (SIDE // 2))
            tops = [None] * SIDE
            for jj in range(NEAR // 2):
                for g, (s, half, q, qb) in enumerate(items):
                    sco = score(q, near_pair(qb, 2 * jj))
                    sc[g, jj] = sco
                    top = jnp.maximum(sco[:, :BLK], sco[:, BLK:])
                    tops[g] = top if jj == 0 else jnp.maximum(tops[g], top)
            tops = [jnp.max(top, axis=1, keepdims=True) for top in tops]
            accs = [None] * SIDE
            for jj in range(NEAR // 2):
                for g, (s, half, q, qb) in enumerate(items):
                    a = weigh(sc[g, jj], tops[g], near_pair(qb, 2 * jj))
                    accs[g] = a if jj == 0 else accs[g] + a
            for g, (s, half, q, qb) in enumerate(items):
                acc_v[i, s, half] = accs[g]
                top_v[i, s, half] = jnp.broadcast_to(tops[g], (BLK, 128))

    def distant(i):
        @pl.loop(0, 2 * SEQ // SIDE)
        def _(t):
            items = items_of(i, t * (SIDE // 2))
            pairs = [[far_pair(qb, 2 * jj) for jj in range(REMOTE // 2)] for _, _, _, qb in items]
            scores, tops, accs = [], [], []
            for g, (s, half, q, qb) in enumerate(items):
                pieces = []
                for jj in range(REMOTE // 2):
                    sco = score(q, pairs[g][jj])
                    for part in range(2):
                        piece = sco[:, part * BLK : (part + 1) * BLK]
                        valid = NEAR + 2 * jj + part < cnt_s[qb]
                        pieces.append(jnp.where(valid, piece, -1e30))
                scores.append(pieces)
            for g, (s, half, q, qb) in enumerate(items):
                m = top_v[i, s, half]
                for piece in scores[g]:
                    m = jnp.maximum(m, piece)
                tops.append(jnp.max(m, axis=1, keepdims=True))
            for g, (s, half, q, qb) in enumerate(items):
                acc = acc_v[i, s, half] * jnp.exp(top_v[i, s, half] - tops[g])
                for jj in range(REMOTE // 2):
                    both = jnp.concatenate(scores[g][2 * jj : 2 * jj + 2], axis=1)
                    acc = acc + weigh(both, tops[g], pairs[g][jj])
                accs.append(acc)
            low = low_lanes((BLK, 128))
            for u in range(SIDE // 2):
                s = items[2 * u][0]
                left, right = accs[2 * u : 2 * u + 2]
                lsw, rsw = swap_halves(left), swap_halves(right)
                value = jnp.where(low, lsw, right)
                total = jnp.where(low, left, rsw)
                outs[i, s] = (value / total).astype(BF16)

            for u in range(SIDE // 2):
                d = t * (SIDE // 2) + u

                @pl.when(d > 0)
                def _(d=d):
                    ret_copy(i, lax.rem(me + d, SEQ), d).start()

    landed(q_own(0), qq(0))
    near(0)
    landed(q_own(1), qq(1))
    near(1)

    for c in range(CH):

        @pl.loop(1, CL)
        def _(d, c=c):
            z_copy(c, d).wait()

    far_copy.wait()
    for i in range(2):
        distant(i)
        ret_own(i).start()

    @pl.loop(1, SEQ)
    def _(d):
        q_copy(1, d).wait_send()

    wo_copy.wait()
    for i in range(2):
        ret_own(i).wait()

        @pl.loop(1, SEQ)
        def _(d, i=i):
            ret_copy(i, lax.rem(me + d, SEQ), d).wait()

        for g in range(HEADS // 2):
            a = ret[i, 2 * g].astype(F32)
            b = ret[i, 2 * g + 1].astype(F32)
            low = low_lanes(a.shape)
            col = slice(g * 128, (g + 1) * 128)
            att[:BLK, col] = jnp.where(low, a, swap_halves(b)).astype(BF16)
            att[BLK:, col] = jnp.where(low, swap_halves(a), b).astype(BF16)
        out = jnp.dot(att[...], wo_v[...], preferred_element_type=F32).astype(BF16)
        o_ref[i] = out[:BLK]
        o_ref[2 + i] = out[BLK:]


def on_device(nodes, w_qkv, w_out, kv_ids, counts):
    vm = pl.BlockSpec(memory_space=pltpu.VMEM)
    sm = pl.BlockSpec(memory_space=pltpu.SMEM)
    hbm = pl.BlockSpec(memory_space=pl.ANY)
    dma = pltpu.SemaphoreType.DMA
    out = pl.pallas_call(
        body,
        out_shape=jax.ShapeDtypeStruct((OWN, BLK, D), BF16),
        in_specs=[sm, sm, vm, vm, hbm, hbm],
        out_specs=vm,
        scratch_shapes=[
            *[pltpu.VMEM((HEADS, OWN, r, 128), BF16) for r in ROWS],
            *[pltpu.VMEM((QB, r, 128), BF16) for r in ROWS],
            *[pltpu.VMEM((CL, REQ, r, 128), BF16) for r in ROWS],
            *[pltpu.VMEM((CL * REQ, r, 128), BF16) for r in ROWS],
            pltpu.VMEM((GROUPS, D, WCOL), BF16),
            pltpu.VMEM((D, D), BF16),
            pltpu.VMEM((HEADS, 2, BLK, 128), BF16),
            pltpu.VMEM((2, SEQ, BLK, 128), BF16),
            pltpu.VMEM((CL, 1, 128), jnp.int32),
            pltpu.VMEM((CL, 1, 128), jnp.int32),
            pltpu.SMEM((CL, 1, 128), jnp.int32),
            pltpu.VMEM((QB, 128), jnp.int32),
            pltpu.SMEM((QB, 128), jnp.int32),
            pltpu.VMEM((SIDE, NEAR // 2, BLK, 2 * BLK), F32),
            pltpu.VMEM((2, SEQ, 2, BLK, 128), F32),
            pltpu.VMEM((2, SEQ, 2, BLK, 128), F32),
            pltpu.VMEM((2, SEQ, BLK, 128), BF16),
            pltpu.VMEM((2, SEQ, BLK, 128), BF16),
            pltpu.VMEM((2 * BLK, D), BF16),
            dma((GROUPS + 1,)),
            dma((CL,)),
            dma((CL,)),
            dma((CH, SEQ)),
            dma((CH, SEQ)),
            dma((2, SEQ)),
            dma((2, SEQ)),
            dma((CH, CL)),
            dma((CH, CL)),
            dma((2, SEQ)),
            dma((2, SEQ)),
            dma((CH + 4,)),
            dma((2,)),
        ],
        compiler_params=pltpu.CompilerParams(
            collective_id=0, has_side_effects=True, vmem_limit_bytes=60 << 20
        ),
        name="sublayer",
    )(kv_ids, counts, nodes, kv_ids, w_qkv, w_out)
    return out.reshape(OWN * BLK, D)


def solution(mesh):
    placed = (P(("cluster", "seq"), None), P(), P(), P("cluster", None), P("cluster"))
    return jax.shard_map(
        on_device,
        mesh=mesh,
        in_specs=placed,
        out_specs=P(("cluster", "seq"), None),
        check_vma=False,
    )
```

```python
import functools

import jax
import jax.numpy as jnp
from jax import lax
from jax.experimental import pallas as pl
from jax.experimental.pallas import tpu as pltpu
from jax.sharding import PartitionSpec as P

D = 1024
HEADS = 16
HD = 64
BLK = 128
KVB = 16
REMOTE = 4
NEAR = KVB - REMOTE
QB = 64
REQ = 16
CL = 8
SEQ = 16
OWN = 4
ROWS = (16, 16, 32, 32, 32)
CH = len(ROWS)
FIRST = tuple(sum(ROWS[:c]) for c in range(CH))
GROUPS = 4
WCOL = 3 * D // GROUPS
SIDE = 8
MESH = pl.DeviceIdType.MESH
F32 = jnp.float32
BF16 = jnp.bfloat16


def low_lanes(shape):
    return lax.broadcasted_iota(jnp.int32, shape, len(shape) - 1) < HD


def swap_halves(x):
    return pltpu.roll(x, HD, x.ndim - 1)


def body(ids_s, cnt_s, nodes, ids_v, w_hbm, wo_hbm, o_ref, *scratch):
    me = lax.axis_index("seq")
    mc = lax.axis_index("cluster")
    scratch = list(scratch)

    def take(n):
        got = scratch[:n]
        del scratch[:n]
        return got

    kvs, kvc, snd, far = take(CH), take(CH), take(CH), take(CH)
    w_v, wo_v, qs, qr, lsend, lrecv, lsm, far_v, far_s, sc, acc_v, top_v, outs, ret, att, turn = take(16)
    w_sem, l_ss, l_rs, kv_ss, kv_rs, q_ss, q_rs, z_ss, z_rs, r_ss, r_rs, own_sem, sm_sem = scratch

    barrier = pltpu.get_barrier_semaphore()

    @pl.loop(1, SEQ)
    def _(d):
        pl.semaphore_signal(barrier, inc=1, device_id={"seq": lax.rem(me + d, SEQ)}, device_id_type=MESH)

    @pl.loop(1, CL)
    def _(d):
        pl.semaphore_signal(barrier, inc=1, device_id={"cluster": lax.rem(mc + d, CL)}, device_id_type=MESH)

    def w_copy(k):
        g = lax.rem(me // GROUPS + k, GROUPS)
        return pltpu.make_async_copy(
            w_hbm.at[:, pl.ds(pl.multiple_of(g * WCOL, 128), WCOL)], w_v.at[k], w_sem.at[k]
        )

    @pl.loop(0, GROUPS)
    def _(k):
        w_copy(k).start()

    wo_copy = pltpu.make_async_copy(wo_hbm, wo_v, w_sem.at[GROUPS])
    wo_copy.start()

    def kv_copy(c, d):
        peer = lax.rem(me + d, SEQ)
        return pltpu.make_async_remote_copy(
            src_ref=kvs[c].at[peer],
            dst_ref=kvc[c].at[pl.ds(OWN * me, OWN)],
            send_sem=kv_ss.at[c, d],
            recv_sem=kv_rs.at[c, d],
            device_id={"seq": peer},
            device_id_type=MESH,
        )

    def kv_own(c):
        return pltpu.make_async_copy(kvs[c].at[me], kvc[c].at[pl.ds(OWN * me, OWN)], own_sem.at[c])

    def q_copy(i, d):
        peer = lax.rem(me + d, SEQ)
        return pltpu.make_async_remote_copy(
            src_ref=qs.at[peer, i],
            dst_ref=qr.at[i, me],
            send_sem=q_ss.at[i, d],
            recv_sem=q_rs.at[i, d],
            device_id={"seq": peer},
            device_id_type=MESH,
        )

    def q_own(i):
        return pltpu.make_async_copy(qs.at[me, i], qr.at[i, me], own_sem.at[CH + i])

    def list_copy(d):
        peer = lax.rem(mc + d, CL)
        return pltpu.make_async_remote_copy(
            src_ref=lsend.at[peer],
            dst_ref=lrecv.at[CL - d],
            send_sem=l_ss.at[d],
            recv_sem=l_rs.at[d],
            device_id={"cluster": peer},
            device_id_type=MESH,
        )

    def z_copy(c, d):
        return pltpu.make_async_remote_copy(
            src_ref=snd[c].at[d],
            dst_ref=far[c].at[pl.ds(REQ * mc, REQ)],
            send_sem=z_ss.at[c, d],
            recv_sem=z_rs.at[c, d],
            device_id={"cluster": lax.rem(mc + d, CL)},
            device_id_type=MESH,
        )

    def ret_copy(i, peer, d):
        return pltpu.make_async_remote_copy(
            src_ref=outs.at[i, peer],
            dst_ref=ret.at[i, me],
            send_sem=r_ss.at[i, d],
            recv_sem=r_rs.at[i, d],
            device_id={"seq": peer},
            device_id_type=MESH,
        )

    def ret_own(i):
        return pltpu.make_async_copy(outs.at[i, me], ret.at[i, me], own_sem.at[CH + 2 + i])

    def start(own, copy):
        own.start()

        @pl.loop(1, SEQ)
        def _(d):
            copy(d).start()

    def start_after(done, own, copy):
        own.start()

        @pl.loop(1, SEQ)
        def _(d):
            done(d).wait_send()
            copy(d).start()

    def landed(own, copy):
        own.wait()

        @pl.loop(1, SEQ)
        def _(d):
            copy(d).wait_recv()

    def kv(c):
        return functools.partial(kv_copy, c)

    def qq(i):
        return functools.partial(q_copy, i)

    def pack(c):
        @pl.loop(1, CL)
        def _(d):
            for r in range(REQ):
                snd[c][d, r] = kvc[c][lsm[d, 0, r] & (QB - 1)]
            z_copy(c, d).start()

    turn[...] = jnp.zeros((128, 128), F32)
    turn[:KVB, :QB] = ids_v[...].astype(F32)
    ids_t = jnp.transpose(turn[...])
    lane = lax.broadcasted_iota(jnp.int32, (QB, CL * QB), 1).astype(F32)
    hits = [ids_t[:QB, NEAR + j : NEAR + j + 1] == lane for j in range(REMOTE)]
    named = jnp.where(hits[0] | hits[1] | hits[2] | hits[3], 1.0, 0.0)
    present = jnp.max(named, axis=0, keepdims=True)
    present = jnp.broadcast_to(present, (8, CL * QB))
    lane8 = lax.broadcasted_iota(jnp.int32, (8, CL * QB), 1)
    inner = lane8 % QB
    rank = present
    step = 1
    while step < QB:
        rank = rank + jnp.where(inner >= step, pltpu.roll(rank, step, 1), 0.0)
        step *= 2
    rank = rank - present
    slot = lax.broadcasted_iota(jnp.int32, (REQ, CL * QB), 0).astype(F32)
    wanted = jnp.where((slot == rank[:1]) & (present[:1] > 0.5), 1.0, 0.0).astype(BF16)
    sub8 = lax.broadcasted_iota(jnp.int32, (CL, CL * QB), 0)
    worth = jnp.where(lane8 // QB == sub8, inner, 0).astype(F32).astype(BF16)
    wanted = jnp.concatenate([wanted, jnp.zeros((128 - REQ, CL * QB), BF16)], axis=0)
    lists = lax.dot_general(
        worth, wanted, (((1,), (1,)), ((), ())), preferred_element_type=F32
    ).astype(jnp.int32)
    for p in range(CL):
        lsend[p] = lists[p : p + 1]
    place = rank + (lane8 // QB * REQ).astype(F32)
    lane_q = lax.broadcasted_iota(jnp.int32, (QB, 128), 1)
    table = jnp.zeros((QB, 128), F32)
    for j in range(REMOTE):
        at = jnp.sum(jnp.where(hits[j], place[:1], 0.0), axis=1, keepdims=True)
        table = jnp.where(lane_q == j, at, table)
    far_v[...] = table.astype(jnp.int32)
    far_copy = pltpu.make_async_copy(far_v, far_s, sm_sem.at[1])
    far_copy.start()

    def project(k, x):
        p = jnp.dot(x, w_v[k], preferred_element_type=F32)
        return [[p[:, 384 * n + 128 * e : 384 * n + 128 * e + 128] for e in range(3)] for n in range(2)]

    def group(k):
        return lax.rem(me // GROUPS + k, GROUPS)

    def send_group(c, k):
        @pl.loop(0, HEADS // GROUPS)
        def _(h):
            d = lax.rem(group(k) * (HEADS // GROUPS) + h + SEQ - me, SEQ)

            @pl.when(d > 0)
            def _():
                kv_copy(c, d).start()

    x0 = jnp.concatenate([nodes[b * BLK : b * BLK + ROWS[0]] for b in range(OWN)], axis=0)

    @pl.loop(0, GROUPS)
    def _(k):
        w_copy(k).wait()
        low = low_lanes((OWN * ROWS[0], 128))
        for n, (t0, t1, t2) in enumerate(project(k, x0)):
            h0 = 4 * group(k) + 2 * n
            kv0 = jnp.where(low, swap_halves(t0), swap_halves(t1))
            kvs[0][h0] = kv0.astype(BF16).reshape(OWN, ROWS[0], 128)
            kvs[0][h0 + 1] = t2.astype(BF16).reshape(OWN, ROWS[0], 128)

        @pl.when(k == 0)
        def _():
            pl.semaphore_wait(barrier, SEQ + CL - 2)

            @pl.loop(1, CL)
            def _(d):
                list_copy(d).start()

        send_group(0, k)

    kv_own(0).start()

    @pl.loop(0, GROUPS)
    def _(k):
        @pl.when(k == GROUPS // 2)
        def _():
            @pl.loop(1, CL)
            def _(d):
                list_copy(d).wait()

            sm_copy = pltpu.make_async_copy(
                lrecv.at[pl.ds(1, CL - 1)], lsm.at[pl.ds(1, CL - 1)], sm_sem.at[0]
            )
            sm_copy.start()
            sm_copy.wait()


            landed(kv_own(0), kv(0))
            pack(0)

        low = low_lanes((OWN * BLK, 128))
        half = OWN * BLK // 2
        scale = HD**-0.5
        for n, (t0, t1, t2) in enumerate(project(k, nodes[...])):
            r0, r1 = swap_halves(t0), swap_halves(t1)
            h0 = 4 * group(k) + 2 * n
            kv0 = jnp.where(low, r0, r1).astype(BF16).reshape(OWN, BLK, 128)
            kv1 = t2.astype(BF16).reshape(OWN, BLK, 128)
            for c in range(1, CH):
                kvs[c][h0] = kv0[:, FIRST[c] : FIRST[c] + ROWS[c]]
                kvs[c][h0 + 1] = kv1[:, FIRST[c] : FIRST[c] + ROWS[c]]
            q0 = jnp.where(low[:half], t0[:half], r0[half:]) * scale
            q1 = jnp.where(low[:half], r1[:half], t1[half:]) * scale
            qs[h0] = q0.astype(BF16).reshape(2, BLK, 128)
            qs[h0 + 1] = q1.astype(BF16).reshape(2, BLK, 128)
        send_group(1, k)

    kv_own(1).start()
    start_after(kv(1), kv_own(2), kv(2))
    for c in range(1, CH):
        landed(kv_own(c), kv(c))
        pack(c)
        if c + 2 < CH:
            start_after(kv(c + 1), kv_own(c + 2), kv(c + 2))
        elif c + 2 == CH:
            start_after(kv(c + 1), q_own(0), qq(0))
    start_after(qq(0), q_own(1), qq(1))

    def block_of(bufs, b):
        return [bufs[c][b] for c in range(CH)]

    def pair_of(bufs, b0, b1):
        return jnp.concatenate(block_of(bufs, b0) + block_of(bufs, b1), axis=0)

    def near_pair(qb, j):
        return pair_of(kvc, ids_s[j, qb] & (QB - 1), ids_s[j + 1, qb] & (QB - 1))

    def far_pair(qb, j):
        last = CL * REQ - 1
        return pair_of(far, far_s[qb, j] & last, far_s[qb, j + 1] & last)

    def score(q, kv):
        return lax.dot_general(q, kv, (((1,), (1,)), ((), ())), preferred_element_type=F32)

    def weigh(s, m, kv):
        p = jnp.exp(s - m).astype(BF16)
        v1 = jnp.where(low_lanes(kv.shape), jnp.ones_like(kv), kv)
        return jnp.dot(p, v1, preferred_element_type=F32)

    def queries(i, s):
        qp = qr[i, s]
        low = low_lanes(qp.shape)
        left = jnp.where(low, qp, jnp.zeros_like(qp))
        right = jnp.where(low, swap_halves(qp.astype(F32)), 0.0).astype(BF16)
        return left, right

    def items_of(i, first):
        items = []
        for u in range(SIDE // 2):
            s = lax.rem(me + first + u, SEQ)
            for half, q in enumerate(queries(i, s)):
                items.append((s, half, q, s * OWN + i + 2 * half))
        return items

    def near(i):
        @pl.loop(0, 2 * SEQ // SIDE)
        def _(t):
            items = items_of(i, t * (SIDE // 2))
            tops = [None] * SIDE
            for jj in range(NEAR // 2):
                for g, (s, half, q, qb) in enumerate(items):
                    sco = score(q, near_pair(qb, 2 * jj))
                    sc[g, jj] = sco
                    top = jnp.maximum(sco[:, :BLK], sco[:, BLK:])
                    tops[g] = top if jj == 0 else jnp.maximum(tops[g], top)
            tops = [jnp.max(top, axis=1, keepdims=True) for top in tops]
            accs = [None] * SIDE
            for jj in range(NEAR // 2):
                for g, (s, half, q, qb) in enumerate(items):
                    a = weigh(sc[g, jj], tops[g], near_pair(qb, 2 * jj))
                    accs[g] = a if jj == 0 else accs[g] + a
            for g, (s, half, q, qb) in enumerate(items):
                acc_v[i, s, half] = accs[g]
                top_v[i, s, half] = jnp.broadcast_to(tops[g], (BLK, 128))

    def distant(i):
        @pl.loop(0, 2 * SEQ // SIDE)
        def _(t):
            items = items_of(i, t * (SIDE // 2))
            pairs = [[far_pair(qb, 2 * jj) for jj in range(REMOTE // 2)] for _, _, _, qb in items]
            scores, tops, accs = [], [], []
            for g, (s, half, q, qb) in enumerate(items):
                pieces = []
                for jj in range(REMOTE // 2):
                    sco = score(q, pairs[g][jj])
                    for part in range(2):
                        piece = sco[:, part * BLK : (part + 1) * BLK]
                        valid = NEAR + 2 * jj + part < cnt_s[qb]
                        pieces.append(jnp.where(valid, piece, -1e30))
                scores.append(pieces)
            for g, (s, half, q, qb) in enumerate(items):
                m = top_v[i, s, half]
                for piece in scores[g]:
                    m = jnp.maximum(m, piece)
                tops.append(jnp.max(m, axis=1, keepdims=True))
            for g, (s, half, q, qb) in enumerate(items):
                acc = acc_v[i, s, half] * jnp.exp(top_v[i, s, half] - tops[g])
                for jj in range(REMOTE // 2):
                    both = jnp.concatenate(scores[g][2 * jj : 2 * jj + 2], axis=1)
                    acc = acc + weigh(both, tops[g], pairs[g][jj])
                accs.append(acc)
            low = low_lanes((BLK, 128))
            for u in range(SIDE // 2):
                s = items[2 * u][0]
                left, right = accs[2 * u : 2 * u + 2]
                lsw, rsw = swap_halves(left), swap_halves(right)
                value = jnp.where(low, lsw, right)
                total = jnp.where(low, left, rsw)
                outs[i, s] = (value / total).astype(BF16)

            for u in range(SIDE // 2):
                d = t * (SIDE // 2) + u

                @pl.when(d > 0)
                def _(d=d):
                    ret_copy(i, lax.rem(me + d, SEQ), d).start()

    landed(q_own(0), qq(0))
    near(0)
    landed(q_own(1), qq(1))
    near(1)

    for c in range(CH):

        @pl.loop(1, CL)
        def _(d, c=c):
            z_copy(c, d).wait()

    far_copy.wait()
    for i in range(2):
        distant(i)
        ret_own(i).start()

    @pl.loop(1, SEQ)
    def _(d):
        q_copy(1, d).wait_send()
        kv_copy(0, d).wait_send()

    wo_copy.wait()
    for i in range(2):
        ret_own(i).wait()

        @pl.loop(1, SEQ)
        def _(d, i=i):
            ret_copy(i, lax.rem(me + d, SEQ), d).wait()

        for g in range(HEADS // 2):
            a = ret[i, 2 * g].astype(F32)
            b = ret[i, 2 * g + 1].astype(F32)
            low = low_lanes(a.shape)
            col = slice(g * 128, (g + 1) * 128)
            att[:BLK, col] = jnp.where(low, a, swap_halves(b)).astype(BF16)
            att[BLK:, col] = jnp.where(low, swap_halves(a), b).astype(BF16)
        out = jnp.dot(att[...], wo_v[...], preferred_element_type=F32).astype(BF16)
        o_ref[i] = out[:BLK]
        o_ref[2 + i] = out[BLK:]


def write_out(x_ref, o_ref, sem):
    copies = [pltpu.make_async_copy(x_ref.at[b], o_ref.at[b], sem.at[b]) for b in range(OWN)]
    for copy in copies:
        copy.start()
    for copy in copies:
        copy.wait()


def on_device(nodes, w_qkv, w_out, kv_ids, counts):
    vm = pl.BlockSpec(memory_space=pltpu.VMEM)
    sm = pl.BlockSpec(memory_space=pltpu.SMEM)
    hbm = pl.BlockSpec(memory_space=pl.ANY)
    dma = pltpu.SemaphoreType.DMA
    out = pl.pallas_call(
        body,
        out_shape=pltpu.VMEM((OWN, BLK, D), BF16),
        in_specs=[sm, sm, vm, vm, hbm, hbm],
        out_specs=vm,
        scratch_shapes=[
            *[pltpu.VMEM((HEADS, OWN, r, 128), BF16) for r in ROWS],
            *[pltpu.VMEM((QB, r, 128), BF16) for r in ROWS],
            *[pltpu.VMEM((CL, REQ, r, 128), BF16) for r in ROWS],
            *[pltpu.VMEM((CL * REQ, r, 128), BF16) for r in ROWS],
            pltpu.VMEM((GROUPS, D, WCOL), BF16),
            pltpu.VMEM((D, D), BF16),
            pltpu.VMEM((HEADS, 2, BLK, 128), BF16),
            pltpu.VMEM((2, SEQ, BLK, 128), BF16),
            pltpu.VMEM((CL, 1, 128), jnp.int32),
            pltpu.VMEM((CL, 1, 128), jnp.int32),
            pltpu.SMEM((CL, 1, 128), jnp.int32),
            pltpu.VMEM((QB, 128), jnp.int32),
            pltpu.SMEM((QB, 128), jnp.int32),
            pltpu.VMEM((SIDE, NEAR // 2, BLK, 2 * BLK), F32),
            pltpu.VMEM((2, SEQ, 2, BLK, 128), F32),
            pltpu.VMEM((2, SEQ, 2, BLK, 128), F32),
            pltpu.VMEM((2, SEQ, BLK, 128), BF16),
            pltpu.VMEM((2, SEQ, BLK, 128), BF16),
            pltpu.VMEM((2 * BLK, D), BF16),
            pltpu.VMEM((128, 128), F32),
            dma((GROUPS + 1,)),
            dma((CL,)),
            dma((CL,)),
            dma((CH, SEQ)),
            dma((CH, SEQ)),
            dma((2, SEQ)),
            dma((2, SEQ)),
            dma((CH, CL)),
            dma((CH, CL)),
            dma((2, SEQ)),
            dma((2, SEQ)),
            dma((CH + 4,)),
            dma((2,)),
        ],
        compiler_params=pltpu.CompilerParams(
            collective_id=0, has_side_effects=True, vmem_limit_bytes=60 << 20
        ),
        name="sublayer",
    )(kv_ids.T, counts, nodes, kv_ids.T, w_qkv, w_out)
    return pl.pallas_call(
        write_out,
        out_shape=jax.ShapeDtypeStruct((OWN, BLK, D), BF16),
        in_specs=[vm],
        out_specs=hbm,
        scratch_shapes=[dma((OWN,))],
        compiler_params=pltpu.CompilerParams(vmem_limit_bytes=1 << 20),
        name="write_out",
    )(out).reshape(OWN * BLK, D)


def solution(mesh):
    placed = (P(("cluster", "seq"), None), P(), P(), P("cluster", None), P("cluster"))
    return jax.shard_map(
        on_device,
        mesh=mesh,
        in_specs=placed,
        out_specs=P(("cluster", "seq"), None),
        check_vma=False,
    )
```

```python
import functools

import jax
import jax.numpy as jnp
from jax import lax
from jax.experimental import pallas as pl
from jax.experimental.pallas import tpu as pltpu
from jax.sharding import PartitionSpec as P

D = 1024
HEADS = 16
HD = 64
BLK = 128
KVB = 16
REMOTE = 4
NEAR = KVB - REMOTE
LEAST = 13
QB = 64
REQ = 16
CL = 8
SEQ = 16
OWN = 4
ROWS = (32, 32, 32, 32)
CH = len(ROWS)
FIRST = tuple(sum(ROWS[:c]) for c in range(CH))
GROUPS = 4
WCOL = 3 * D // GROUPS
SIDE = 8
WIDE = 16
MESH = pl.DeviceIdType.MESH
F32 = jnp.float32
BF16 = jnp.bfloat16


def low_lanes(shape):
    return lax.broadcasted_iota(jnp.int32, shape, len(shape) - 1) < HD


def swap_halves(x):
    return pltpu.roll(x, HD, x.ndim - 1)


def body(ids_s, cnt_s, nodes_hbm, ids_hbm, w_hbm, wo_hbm, o_ref, *scratch):
    me = lax.axis_index("seq")
    mc = lax.axis_index("cluster")
    scratch = list(scratch)

    def take(n):
        got = scratch[:n]
        del scratch[:n]
        return got

    kvs, kvc, snd, far = take(CH), take(CH), take(CH), take(CH)
    w_v, wo_v, qs, qr, lsend, lrecv, lsm, far_v, far_s, sc, acc_v, top_v, outs, ret, att, turn, nodes, ids_v = take(18)
    w_sem, l_ss, l_rs, kv_ss, kv_rs, q_ss, q_rs, z_ss, z_rs, r_ss, r_rs, own_sem, sm_sem = scratch

    barrier = pltpu.get_barrier_semaphore()

    for d in range(1, SEQ):
        pl.semaphore_signal(barrier, inc=1, device_id={"seq": lax.rem(me + d, SEQ)}, device_id_type=MESH)
    for d in range(1, CL):
        pl.semaphore_signal(barrier, inc=1, device_id={"cluster": lax.rem(mc + d, CL)}, device_id_type=MESH)

    ids_copy = pltpu.make_async_copy(ids_hbm, ids_v, sm_sem.at[2])
    ids_copy.start()
    nodes_copy = pltpu.make_async_copy(nodes_hbm, nodes, sm_sem.at[3])
    nodes_copy.start()

    def w_copy(k):
        g = lax.rem(me // GROUPS + k, GROUPS)
        return pltpu.make_async_copy(
            w_hbm.at[:, pl.ds(pl.multiple_of(g * WCOL, 128), WCOL)], w_v.at[k], w_sem.at[k]
        )

    @pl.loop(0, GROUPS)
    def _(k):
        w_copy(k).start()

    wo_copy = pltpu.make_async_copy(wo_hbm, wo_v, w_sem.at[GROUPS])
    def kv_copy(c, d):
        peer = lax.rem(me + d, SEQ)
        return pltpu.make_async_remote_copy(
            src_ref=kvs[c].at[peer],
            dst_ref=kvc[c].at[pl.ds(OWN * me, OWN)],
            send_sem=kv_ss.at[c, d],
            recv_sem=kv_rs.at[c, d],
            device_id={"seq": peer},
            device_id_type=MESH,
        )

    def kv_own(c):
        return pltpu.make_async_copy(kvs[c].at[me], kvc[c].at[pl.ds(OWN * me, OWN)], own_sem.at[c])

    def q_copy(i, d):
        peer = lax.rem(me + d, SEQ)
        return pltpu.make_async_remote_copy(
            src_ref=qs.at[peer, i],
            dst_ref=qr.at[i, me],
            send_sem=q_ss.at[i, d],
            recv_sem=q_rs.at[i, d],
            device_id={"seq": peer},
            device_id_type=MESH,
        )

    def q_own(i):
        return pltpu.make_async_copy(qs.at[me, i], qr.at[i, me], own_sem.at[CH + i])

    def list_copy(d):
        peer = lax.rem(mc + d, CL)
        return pltpu.make_async_remote_copy(
            src_ref=lsend.at[peer],
            dst_ref=lrecv.at[CL - d],
            send_sem=l_ss.at[d],
            recv_sem=l_rs.at[d],
            device_id={"cluster": peer},
            device_id_type=MESH,
        )

    def z_copy(c, d):
        return pltpu.make_async_remote_copy(
            src_ref=snd[c].at[d],
            dst_ref=far[c].at[pl.ds(REQ * mc, REQ)],
            send_sem=z_ss.at[c, d],
            recv_sem=z_rs.at[c, d],
            device_id={"cluster": lax.rem(mc + d, CL)},
            device_id_type=MESH,
        )

    def ret_copy(i, peer, d):
        return pltpu.make_async_remote_copy(
            src_ref=outs.at[i, peer],
            dst_ref=ret.at[i, me],
            send_sem=r_ss.at[i, d],
            recv_sem=r_rs.at[i, d],
            device_id={"seq": peer},
            device_id_type=MESH,
        )

    def ret_own(i):
        return pltpu.make_async_copy(outs.at[i, me], ret.at[i, me], own_sem.at[CH + 2 + i])

    def start(own, copy):
        own.start()

        @pl.loop(1, SEQ)
        def _(d):
            copy(d).start()

    def start_after(done, own, copy):
        own.start()

        @pl.loop(1, SEQ)
        def _(d):
            done(d).wait_send()
            copy(d).start()

    def landed(own, copy):
        own.wait()

        @pl.loop(1, SEQ)
        def _(d):
            copy(d).wait_recv()

    def kv(c):
        return functools.partial(kv_copy, c)

    def qq(i):
        return functools.partial(q_copy, i)

    def pack(c):
        @pl.loop(1, CL)
        def _(d):
            for r in range(REQ):
                snd[c][d, r] = kvc[c][lsm[d, 0, r] & (QB - 1)]
            z_copy(c, d).start()

    turn[...] = jnp.zeros((128, 128), F32)
    ids_copy.wait()
    turn[:KVB, :QB] = ids_v[...].astype(F32)
    ids_t = jnp.transpose(turn[...])
    lane = lax.broadcasted_iota(jnp.int32, (QB, CL * QB), 1).astype(F32)
    hits = [ids_t[:QB, NEAR + j : NEAR + j + 1] == lane for j in range(REMOTE)]
    named = jnp.where(hits[0] | hits[1] | hits[2] | hits[3], 1.0, 0.0)
    present = jnp.max(named, axis=0, keepdims=True)
    present = jnp.broadcast_to(present, (8, CL * QB))
    lane8 = lax.broadcasted_iota(jnp.int32, (8, CL * QB), 1)
    inner = lane8 % QB
    rank = present
    step = 1
    while step < QB:
        rank = rank + jnp.where(inner >= step, pltpu.roll(rank, step, 1), 0.0)
        step *= 2
    rank = rank - present
    slot = lax.broadcasted_iota(jnp.int32, (REQ, CL * QB), 0).astype(F32)
    wanted = jnp.where((slot == rank[:1]) & (present[:1] > 0.5), 1.0, 0.0).astype(BF16)
    sub8 = lax.broadcasted_iota(jnp.int32, (CL, CL * QB), 0)
    worth = jnp.where(lane8 // QB == sub8, inner, 0).astype(F32).astype(BF16)
    wanted = jnp.concatenate([wanted, jnp.zeros((128 - REQ, CL * QB), BF16)], axis=0)
    lists = lax.dot_general(
        worth, wanted, (((1,), (1,)), ((), ())), preferred_element_type=F32
    ).astype(jnp.int32)
    for p in range(CL):
        lsend[p] = lists[p : p + 1]
    place = rank + (lane8 // QB * REQ).astype(F32)
    lane_q = lax.broadcasted_iota(jnp.int32, (QB, 128), 1)
    table = jnp.zeros((QB, 128), F32)
    for j in range(REMOTE):
        at = jnp.sum(jnp.where(hits[j], place[:1], 0.0), axis=1, keepdims=True)
        table = jnp.where(lane_q == j, at, table)
    far_v[...] = table.astype(jnp.int32)
    far_copy = pltpu.make_async_copy(far_v, far_s, sm_sem.at[1])
    far_copy.start()

    def project(k, x):
        p = jnp.dot(x, w_v[k], preferred_element_type=F32)
        return [[p[:, 384 * n + 128 * e : 384 * n + 128 * e + 128] for e in range(3)] for n in range(2)]

    def group(k):
        return lax.rem(me // GROUPS + k, GROUPS)

    nodes_copy.wait()
    x0 = jnp.concatenate([nodes[b * BLK : b * BLK + ROWS[0]] for b in range(OWN)], axis=0)

    @pl.loop(0, GROUPS)
    def _(k):
        w_copy(k).wait()
        low = low_lanes((OWN * ROWS[0], 128))
        for n, (t0, t1, t2) in enumerate(project(k, x0)):
            h0 = 4 * group(k) + 2 * n
            kv0 = jnp.where(low, swap_halves(t0), swap_halves(t1))
            kvs[0][h0] = kv0.astype(BF16).reshape(OWN, ROWS[0], 128)
            kvs[0][h0 + 1] = t2.astype(BF16).reshape(OWN, ROWS[0], 128)

    pl.semaphore_wait(barrier, SEQ + CL - 2)
    for d in range(1, CL):
        list_copy(d).start()
    for d in range(1, SEQ):
        kv_copy(0, d).start()
    kv_own(0).start()
    wo_copy.start()

    @pl.loop(0, GROUPS)
    def _(k):
        low = low_lanes((OWN * BLK, 128))
        half = OWN * BLK // 2
        scale = HD**-0.5
        for n, (t0, t1, t2) in enumerate(project(k, nodes[...])):
            r0, r1 = swap_halves(t0), swap_halves(t1)
            h0 = 4 * group(k) + 2 * n
            kv0 = jnp.where(low, r0, r1).astype(BF16).reshape(OWN, BLK, 128)
            kv1 = t2.astype(BF16).reshape(OWN, BLK, 128)
            for c in range(1, CH):
                kvs[c][h0] = kv0[:, FIRST[c] : FIRST[c] + ROWS[c]]
                kvs[c][h0 + 1] = kv1[:, FIRST[c] : FIRST[c] + ROWS[c]]
            q0 = jnp.where(low[:half], t0[:half], r0[half:]) * scale
            q1 = jnp.where(low[:half], r1[:half], t1[half:]) * scale
            qs[h0] = q0.astype(BF16).reshape(2, BLK, 128)
            qs[h0 + 1] = q1.astype(BF16).reshape(2, BLK, 128)

    start_after(kv(0), kv_own(1), kv(1))
    @pl.loop(1, CL)
    def _(d):
        list_copy(d).wait()

    sm_copy = pltpu.make_async_copy(
        lrecv.at[pl.ds(1, CL - 1)], lsm.at[pl.ds(1, CL - 1)], sm_sem.at[0]
    )
    sm_copy.start()
    sm_copy.wait()

    for c in range(CH):
        landed(kv_own(c), kv(c))
        pack(c)
        if c + 2 < CH:
            start_after(kv(c + 1), kv_own(c + 2), kv(c + 2))
        elif c + 2 == CH:
            start_after(kv(c + 1), q_own(0), qq(0))
    start_after(qq(0), q_own(1), qq(1))

    def block_of(bufs, b):
        return [bufs[c][b] for c in range(CH)]

    def pair_of(bufs, b0, b1):
        return jnp.concatenate(block_of(bufs, b0) + block_of(bufs, b1), axis=0)

    def near_pair(qb, j):
        return pair_of(kvc, ids_s[j, qb] & (QB - 1), ids_s[j + 1, qb] & (QB - 1))

    def far_pair(qb, j):
        last = CL * REQ - 1
        return pair_of(far, far_s[qb, j] & last, far_s[qb, j + 1] & last)

    def score(q, kv):
        return lax.dot_general(q, kv, (((1,), (1,)), ((), ())), preferred_element_type=F32)

    def weigh(s, m, kv):
        p = jnp.exp(s - m).astype(BF16)
        v1 = jnp.where(low_lanes(kv.shape), jnp.ones_like(kv), kv)
        return jnp.dot(p, v1, preferred_element_type=F32)

    def queries(i, s):
        qp = qr[i, s]
        low = low_lanes(qp.shape)
        left = jnp.where(low, qp, jnp.zeros_like(qp))
        right = jnp.where(low, swap_halves(qp.astype(F32)), 0.0).astype(BF16)
        return left, right

    def items_of(i, first, count):
        items = []
        for u in range(count // 2):
            s = lax.rem(me + first + u, SEQ)
            for half, q in enumerate(queries(i, s)):
                items.append((s, half, q, s * OWN + i + 2 * half))
        return items

    def near(i):
        @pl.loop(0, 2 * SEQ // WIDE)
        def _(t):
            items = items_of(i, t * (WIDE // 2), WIDE)
            tops = [None] * WIDE
            for jj in range(NEAR // 2):
                for g, (s, half, q, qb) in enumerate(items):
                    sco = score(q, near_pair(qb, 2 * jj))
                    sc[g, jj] = sco
                    top = jnp.maximum(sco[:, :BLK], sco[:, BLK:])
                    tops[g] = top if jj == 0 else jnp.maximum(tops[g], top)
            tops = [jnp.max(top, axis=1, keepdims=True) for top in tops]
            accs = [None] * WIDE
            for jj in range(NEAR // 2):
                for g, (s, half, q, qb) in enumerate(items):
                    a = weigh(sc[g, jj], tops[g], near_pair(qb, 2 * jj))
                    accs[g] = a if jj == 0 else accs[g] + a
            for g, (s, half, q, qb) in enumerate(items):
                acc_v[i, s, half] = accs[g]
                top_v[i, s, half] = jnp.broadcast_to(tops[g], (BLK, 128))

    def distant(i):
        @pl.loop(0, 2 * SEQ // SIDE)
        def _(t):
            items = items_of(i, t * (SIDE // 2), SIDE)
            pairs = [[far_pair(qb, 2 * jj) for jj in range(REMOTE // 2)] for _, _, _, qb in items]
            scores, tops, accs = [], [], []
            for g, (s, half, q, qb) in enumerate(items):
                pieces = []
                for jj in range(REMOTE // 2):
                    sco = score(q, pairs[g][jj])
                    for part in range(2):
                        piece = sco[:, part * BLK : (part + 1) * BLK]
                        slot = NEAR + 2 * jj + part
                        if slot >= LEAST:
                            piece = jnp.where(slot < cnt_s[qb], piece, -1e30)
                        pieces.append(piece)
                scores.append(pieces)
            for g, (s, half, q, qb) in enumerate(items):
                m = top_v[i, s, half]
                for piece in scores[g]:
                    m = jnp.maximum(m, piece)
                tops.append(jnp.max(m, axis=1, keepdims=True))
            for g, (s, half, q, qb) in enumerate(items):
                acc = acc_v[i, s, half] * jnp.exp(top_v[i, s, half] - tops[g])
                for jj in range(REMOTE // 2):
                    both = jnp.concatenate(scores[g][2 * jj : 2 * jj + 2], axis=1)
                    acc = acc + weigh(both, tops[g], pairs[g][jj])
                accs.append(acc)
            low = low_lanes((BLK, 128))
            for u in range(SIDE // 2):
                s = items[2 * u][0]
                left, right = accs[2 * u : 2 * u + 2]
                lsw, rsw = swap_halves(left), swap_halves(right)
                value = jnp.where(low, lsw, right)
                total = jnp.where(low, left, rsw)
                outs[i, s] = (value / total).astype(BF16)

            for u in range(SIDE // 2):
                d = t * (SIDE // 2) + u

                @pl.when(d > 0)
                def _(d=d):
                    ret_copy(i, lax.rem(me + d, SEQ), d).start()

    landed(q_own(0), qq(0))
    near(0)
    landed(q_own(1), qq(1))
    near(1)

    for c in range(CH):

        @pl.loop(1, CL)
        def _(d, c=c):
            z_copy(c, d).wait()

    far_copy.wait()
    for i in range(2):
        distant(i)
        ret_own(i).start()

    @pl.loop(1, SEQ)
    def _(d):
        q_copy(1, d).wait_send()

    wo_copy.wait()
    for i in range(2):
        ret_own(i).wait()

        @pl.loop(1, SEQ)
        def _(d, i=i):
            ret_copy(i, lax.rem(me + d, SEQ), d).wait()

        for g in range(HEADS // 2):
            a = ret[i, 2 * g].astype(F32)
            b = ret[i, 2 * g + 1].astype(F32)
            low = low_lanes(a.shape)
            col = slice(g * 128, (g + 1) * 128)
            att[:BLK, col] = jnp.where(low, a, swap_halves(b)).astype(BF16)
            att[BLK:, col] = jnp.where(low, swap_halves(a), b).astype(BF16)
        out = jnp.dot(att[...], wo_v[...], preferred_element_type=F32).astype(BF16)
        o_ref[i] = out[:BLK]
        o_ref[2 + i] = out[BLK:]


def write_out(x_ref, o_ref, sem):
    copies = [pltpu.make_async_copy(x_ref.at[b], o_ref.at[b], sem.at[b]) for b in range(OWN)]
    for copy in copies:
        copy.start()
    for copy in copies:
        copy.wait()


def on_device(nodes, w_qkv, w_out, kv_ids, counts):
    vm = pl.BlockSpec(memory_space=pltpu.VMEM)
    sm = pl.BlockSpec(memory_space=pltpu.SMEM)
    hbm = pl.BlockSpec(memory_space=pl.ANY)
    dma = pltpu.SemaphoreType.DMA
    out = pl.pallas_call(
        body,
        out_shape=pltpu.VMEM((OWN, BLK, D), BF16),
        in_specs=[sm, sm, hbm, hbm, hbm, hbm],
        out_specs=vm,
        scratch_shapes=[
            *[pltpu.VMEM((HEADS, OWN, r, 128), BF16) for r in ROWS],
            *[pltpu.VMEM((QB, r, 128), BF16) for r in ROWS],
            *[pltpu.VMEM((CL, REQ, r, 128), BF16) for r in ROWS],
            *[pltpu.VMEM((CL * REQ, r, 128), BF16) for r in ROWS],
            pltpu.VMEM((GROUPS, D, WCOL), BF16),
            pltpu.VMEM((D, D), BF16),
            pltpu.VMEM((HEADS, 2, BLK, 128), BF16),
            pltpu.VMEM((2, SEQ, BLK, 128), BF16),
            pltpu.VMEM((CL, 1, 128), jnp.int32),
            pltpu.VMEM((CL, 1, 128), jnp.int32),
            pltpu.SMEM((CL, 1, 128), jnp.int32),
            pltpu.VMEM((QB, 128), jnp.int32),
            pltpu.SMEM((QB, 128), jnp.int32),
            pltpu.VMEM((WIDE, NEAR // 2, BLK, 2 * BLK), F32),
            pltpu.VMEM((2, SEQ, 2, BLK, 128), F32),
            pltpu.VMEM((2, SEQ, 2, BLK, 128), F32),
            pltpu.VMEM((2, SEQ, BLK, 128), BF16),
            pltpu.VMEM((2, SEQ, BLK, 128), BF16),
            pltpu.VMEM((2 * BLK, D), BF16),
            pltpu.VMEM((128, 128), F32),
            pltpu.VMEM((OWN * BLK, D), BF16),
            pltpu.VMEM((KVB, QB), jnp.int32),
            dma((GROUPS + 1,)),
            dma((CL,)),
            dma((CL,)),
            dma((CH, SEQ)),
            dma((CH, SEQ)),
            dma((2, SEQ)),
            dma((2, SEQ)),
            dma((CH, CL)),
            dma((CH, CL)),
            dma((2, SEQ)),
            dma((2, SEQ)),
            dma((CH + 4,)),
            dma((4,)),
        ],
        compiler_params=pltpu.CompilerParams(
            collective_id=0, has_side_effects=True, vmem_limit_bytes=60 << 20
        ),
        name="sublayer",
    )(kv_ids.T, counts, nodes, kv_ids.T, w_qkv, w_out)
    return pl.pallas_call(
        write_out,
        out_shape=jax.ShapeDtypeStruct((OWN, BLK, D), BF16),
        in_specs=[vm],
        out_specs=hbm,
        scratch_shapes=[dma((OWN,))],
        compiler_params=pltpu.CompilerParams(vmem_limit_bytes=1 << 20),
        name="write_out",
    )(out).reshape(OWN * BLK, D)


def solution(mesh):
    placed = (P(("cluster", "seq"), None), P(), P(), P("cluster", None), P("cluster"))
    return jax.shard_map(
        on_device,
        mesh=mesh,
        in_specs=placed,
        out_specs=P(("cluster", "seq"), None),
        check_vma=False,
    )
```

```python
import functools

import jax
import jax.numpy as jnp
from jax import lax
from jax.experimental import pallas as pl
from jax.experimental.pallas import tpu as pltpu
from jax.sharding import PartitionSpec as P

D = 1024
HEADS = 16
HD = 64
BLK = 128
KVB = 16
REMOTE = 4
NEAR = KVB - REMOTE
QB = 64
REQ = 16
CL = 8
SEQ = 16
OWN = 4
ROWS = (32, 32, 32, 32)
CH = len(ROWS)
FIRST = tuple(sum(ROWS[:c]) for c in range(CH))
GROUPS = 4
WCOL = 3 * D // GROUPS
SIDE = 8
WIDE = 16
MESH = pl.DeviceIdType.MESH
F32 = jnp.float32
BF16 = jnp.bfloat16


def low_lanes(shape):
    return lax.broadcasted_iota(jnp.int32, shape, len(shape) - 1) < HD


def swap_halves(x):
    return pltpu.roll(x, HD, x.ndim - 1)


def body(ids_s, cnt_s, nodes_hbm, ids_hbm, w_hbm, wo_hbm, o_ref, *scratch):
    me = lax.axis_index("seq")
    mc = lax.axis_index("cluster")
    scratch = list(scratch)

    def take(n):
        got = scratch[:n]
        del scratch[:n]
        return got

    kvs, kvc, snd, far = take(CH), take(CH), take(CH), take(CH)
    w_v, wo_v, qs, qr, lsend, lrecv, lsm, far_v, far_s, sc, acc_v, top_v, outs, ret, att, turn, nodes, ids_v = take(18)
    w_sem, l_ss, l_rs, kv_ss, kv_rs, q_ss, q_rs, z_ss, z_rs, r_ss, r_rs, own_sem, sm_sem = scratch

    barrier = pltpu.get_barrier_semaphore()

    for d in range(1, SEQ):
        pl.semaphore_signal(barrier, inc=1, device_id={"seq": lax.rem(me + d, SEQ)}, device_id_type=MESH)
    for d in range(1, CL):
        pl.semaphore_signal(barrier, inc=1, device_id={"cluster": lax.rem(mc + d, CL)}, device_id_type=MESH)

    ids_copy = pltpu.make_async_copy(ids_hbm, ids_v, sm_sem.at[2])
    ids_copy.start()
    nodes_copy = pltpu.make_async_copy(nodes_hbm, nodes, sm_sem.at[3])
    nodes_copy.start()

    def w_copy(k):
        g = lax.rem(me // GROUPS + k, GROUPS)
        return pltpu.make_async_copy(
            w_hbm.at[:, pl.ds(pl.multiple_of(g * WCOL, 128), WCOL)], w_v.at[k], w_sem.at[k]
        )

    @pl.loop(0, GROUPS)
    def _(k):
        w_copy(k).start()

    wo_copy = pltpu.make_async_copy(wo_hbm, wo_v, w_sem.at[GROUPS])
    def kv_copy(c, d):
        peer = lax.rem(me + d, SEQ)
        return pltpu.make_async_remote_copy(
            src_ref=kvs[c].at[peer],
            dst_ref=kvc[c].at[pl.ds(OWN * me, OWN)],
            send_sem=kv_ss.at[c, d],
            recv_sem=kv_rs.at[c, d],
            device_id={"seq": peer},
            device_id_type=MESH,
        )

    def kv_own(c):
        return pltpu.make_async_copy(kvs[c].at[me], kvc[c].at[pl.ds(OWN * me, OWN)], own_sem.at[c])

    def q_copy(i, d):
        peer = lax.rem(me + d, SEQ)
        return pltpu.make_async_remote_copy(
            src_ref=qs.at[peer, i],
            dst_ref=qr.at[i, me],
            send_sem=q_ss.at[i, d],
            recv_sem=q_rs.at[i, d],
            device_id={"seq": peer},
            device_id_type=MESH,
        )

    def q_own(i):
        return pltpu.make_async_copy(qs.at[me, i], qr.at[i, me], own_sem.at[CH + i])

    def list_copy(d):
        peer = lax.rem(mc + d, CL)
        return pltpu.make_async_remote_copy(
            src_ref=lsend.at[peer],
            dst_ref=lrecv.at[CL - d],
            send_sem=l_ss.at[d],
            recv_sem=l_rs.at[d],
            device_id={"cluster": peer},
            device_id_type=MESH,
        )

    def z_copy(c, d):
        return pltpu.make_async_remote_copy(
            src_ref=snd[c].at[d],
            dst_ref=far[c].at[pl.ds(REQ * mc, REQ)],
            send_sem=z_ss.at[c, d],
            recv_sem=z_rs.at[c, d],
            device_id={"cluster": lax.rem(mc + d, CL)},
            device_id_type=MESH,
        )

    def ret_copy(i, peer, d):
        return pltpu.make_async_remote_copy(
            src_ref=outs.at[i, peer],
            dst_ref=ret.at[i, me],
            send_sem=r_ss.at[i, d],
            recv_sem=r_rs.at[i, d],
            device_id={"seq": peer},
            device_id_type=MESH,
        )

    def ret_own(i):
        return pltpu.make_async_copy(outs.at[i, me], ret.at[i, me], own_sem.at[CH + 2 + i])

    def start(own, copy):
        own.start()

        @pl.loop(1, SEQ)
        def _(d):
            copy(d).start()

    def start_after(done, own, copy):
        own.start()

        @pl.loop(1, SEQ)
        def _(d):
            done(d).wait_send()
            copy(d).start()

    def landed(own, copy):
        own.wait()

        @pl.loop(1, SEQ)
        def _(d):
            copy(d).wait_recv()

    def kv(c):
        return functools.partial(kv_copy, c)

    def qq(i):
        return functools.partial(q_copy, i)

    def pack(c):
        @pl.loop(1, CL)
        def _(d):
            for r in range(REQ):
                snd[c][d, r] = kvc[c][lsm[d, 0, r] & (QB - 1)]
            z_copy(c, d).start()

    turn[...] = jnp.zeros((128, 128), F32)
    ids_copy.wait()
    turn[:KVB, :QB] = ids_v[...].astype(F32)
    ids_t = jnp.transpose(turn[...])
    lane = lax.broadcasted_iota(jnp.int32, (QB, CL * QB), 1).astype(F32)
    hits = [ids_t[:QB, NEAR + j : NEAR + j + 1] == lane for j in range(REMOTE)]
    named = jnp.where(hits[0] | hits[1] | hits[2] | hits[3], 1.0, 0.0)
    present = jnp.max(named, axis=0, keepdims=True)
    present = jnp.broadcast_to(present, (8, CL * QB))
    lane8 = lax.broadcasted_iota(jnp.int32, (8, CL * QB), 1)
    inner = lane8 % QB
    rank = present
    step = 1
    while step < QB:
        rank = rank + jnp.where(inner >= step, pltpu.roll(rank, step, 1), 0.0)
        step *= 2
    rank = rank - present
    slot = lax.broadcasted_iota(jnp.int32, (REQ, CL * QB), 0).astype(F32)
    wanted = jnp.where((slot == rank[:1]) & (present[:1] > 0.5), 1.0, 0.0).astype(BF16)
    sub8 = lax.broadcasted_iota(jnp.int32, (CL, CL * QB), 0)
    worth = jnp.where(lane8 // QB == sub8, inner, 0).astype(F32).astype(BF16)
    wanted = jnp.concatenate([wanted, jnp.zeros((128 - REQ, CL * QB), BF16)], axis=0)
    lists = lax.dot_general(
        worth, wanted, (((1,), (1,)), ((), ())), preferred_element_type=F32
    ).astype(jnp.int32)
    for p in range(CL):
        lsend[p] = lists[p : p + 1]
    place = rank + (lane8 // QB * REQ).astype(F32)
    lane_q = lax.broadcasted_iota(jnp.int32, (QB, 128), 1)
    table = jnp.zeros((QB, 128), F32)
    for j in range(REMOTE):
        at = jnp.sum(jnp.where(hits[j], place[:1], 0.0), axis=1, keepdims=True)
        table = jnp.where(lane_q == j, at, table)
    far_v[...] = table.astype(jnp.int32)
    far_copy = pltpu.make_async_copy(far_v, far_s, sm_sem.at[1])
    far_copy.start()

    def project(k, x):
        p = jnp.dot(x, w_v[k], preferred_element_type=F32)
        return [[p[:, 384 * n + 128 * e : 384 * n + 128 * e + 128] for e in range(3)] for n in range(2)]

    def group(k):
        return lax.rem(me // GROUPS + k, GROUPS)

    nodes_copy.wait()
    x0 = jnp.concatenate([nodes[b * BLK : b * BLK + ROWS[0]] for b in range(OWN)], axis=0)

    @pl.loop(0, GROUPS)
    def _(k):
        w_copy(k).wait()
        low = low_lanes((OWN * ROWS[0], 128))
        for n, (t0, t1, t2) in enumerate(project(k, x0)):
            h0 = 4 * group(k) + 2 * n
            kv0 = jnp.where(low, swap_halves(t0), swap_halves(t1))
            kvs[0][h0] = kv0.astype(BF16).reshape(OWN, ROWS[0], 128)
            kvs[0][h0 + 1] = t2.astype(BF16).reshape(OWN, ROWS[0], 128)

    pl.semaphore_wait(barrier, SEQ + CL - 2)
    for d in range(1, CL):
        list_copy(d).start()
    for d in range(1, SEQ):
        kv_copy(0, d).start()
    kv_own(0).start()
    wo_copy.start()

    @pl.loop(0, GROUPS)
    def _(k):
        low = low_lanes((OWN * BLK, 128))
        half = OWN * BLK // 2
        scale = HD**-0.5
        for n, (t0, t1, t2) in enumerate(project(k, nodes[...])):
            r0, r1 = swap_halves(t0), swap_halves(t1)
            h0 = 4 * group(k) + 2 * n
            kv0 = jnp.where(low, r0, r1).astype(BF16).reshape(OWN, BLK, 128)
            kv1 = t2.astype(BF16).reshape(OWN, BLK, 128)
            for c in range(1, CH):
                kvs[c][h0] = kv0[:, FIRST[c] : FIRST[c] + ROWS[c]]
                kvs[c][h0 + 1] = kv1[:, FIRST[c] : FIRST[c] + ROWS[c]]
            q0 = jnp.where(low[:half], t0[:half], r0[half:]) * scale
            q1 = jnp.where(low[:half], r1[:half], t1[half:]) * scale
            qs[h0] = q0.astype(BF16).reshape(2, BLK, 128)
            qs[h0 + 1] = q1.astype(BF16).reshape(2, BLK, 128)

    start_after(kv(0), kv_own(1), kv(1))
    @pl.loop(1, CL)
    def _(d):
        list_copy(d).wait()

    sm_copy = pltpu.make_async_copy(
        lrecv.at[pl.ds(1, CL - 1)], lsm.at[pl.ds(1, CL - 1)], sm_sem.at[0]
    )
    sm_copy.start()
    sm_copy.wait()

    def near_keys(qb, jj, chunks):
        blocks = [ids_s[4 * jj + e, qb] & (QB - 1) for e in range(4)]
        return jnp.concatenate([kvc[c][b] for b in blocks for c in chunks], axis=0)

    def far_keys(qb, jj, chunks):
        blocks = [far_s[qb, 4 * jj + e] & (CL * REQ - 1) for e in range(4)]
        return jnp.concatenate([far[c][b] for b in blocks for c in chunks], axis=0)

    def score(q, kv):
        return lax.dot_general(q, kv, (((1,), (1,)), ((), ())), preferred_element_type=F32)

    def weigh(s, m, kv):
        p = jnp.exp(s - m).astype(BF16)
        v1 = jnp.where(low_lanes(kv.shape), jnp.ones_like(kv), kv)
        return jnp.dot(p, v1, preferred_element_type=F32)

    def queries(i, s):
        qp = qr[i, s]
        low = low_lanes(qp.shape)
        left = jnp.where(low, qp, jnp.zeros_like(qp))
        right = jnp.where(low, swap_halves(qp.astype(F32)), 0.0).astype(BF16)
        return left, right

    def items_of(i, first, count):
        items = []
        for u in range(count // 2):
            s = lax.rem(me + first + u, SEQ)
            for half, q in enumerate(queries(i, s)):
                items.append((s, half, q, s * OWN + i + 2 * half))
        return items

    def attend(i, begin, count, keys, tiles, chunks):
        remote, first = keys is far_keys, keys is near_keys and chunks[0] == 0
        items = items_of(i, begin, count)
        tops, accs = [None] * count, [None] * count
        for jj in range(tiles):
            for g, (s, half, q, qb) in enumerate(items):
                sco = score(q, keys(qb, jj, chunks))
                if remote:
                    lanes = lax.broadcasted_iota(jnp.int32, sco.shape, 1)
                    sco = jnp.where(lanes < (cnt_s[qb] - NEAR) * (2 * BLK // REMOTE), sco, -1e30)
                sc[g, jj] = sco
                top = jnp.maximum(sco[:, :BLK], sco[:, BLK:])
                tops[g] = top if jj == 0 else jnp.maximum(tops[g], top)
        for g, (s, half, q, qb) in enumerate(items):
            top = tops[g] if first else jnp.maximum(tops[g], top_v[i, s, half])
            tops[g] = jnp.max(top, axis=1, keepdims=True)
        for jj in range(tiles):
            for g, (s, half, q, qb) in enumerate(items):
                a = weigh(sc[g, jj], tops[g], keys(qb, jj, chunks))
                accs[g] = a if jj == 0 else accs[g] + a
        for g, (s, half, q, qb) in enumerate(items):
            if not first:
                accs[g] = accs[g] + acc_v[i, s, half] * jnp.exp(top_v[i, s, half] - tops[g])
            if not (remote and chunks[-1] == CH - 1):
                acc_v[i, s, half] = accs[g]
                top_v[i, s, half] = jnp.broadcast_to(tops[g], (BLK, 128))
        return items, accs

    early, late = (0, 1), (2, 3)

    def near(i, chunks):
        @pl.loop(0, 2 * SEQ // WIDE)
        def _(t):
            attend(i, t * (WIDE // 2), WIDE, near_keys, NEAR // 4, chunks)

    for c in range(2):
        landed(kv_own(c), kv(c))
        pack(c)
        if c == 0:
            start_after(kv(1), q_own(0), qq(0))
        else:
            start_after(qq(0), kv_own(2), kv(2))
    landed(q_own(0), qq(0))
    near(0, early)
    start_after(kv(2), q_own(1), qq(1))
    landed(kv_own(2), kv(2))
    pack(2)
    start_after(qq(1), kv_own(3), kv(3))
    landed(q_own(1), qq(1))
    near(1, early)
    landed(kv_own(3), kv(3))
    pack(3)

    @pl.loop(0, 2)
    def _(i):
        near(i, late)

    far_copy.wait()

    def arrived(c):
        @pl.loop(1, CL)
        def _(d):
            z_copy(c, d).wait()

    arrived(0)
    arrived(1)

    @pl.loop(0, 4 * SEQ // WIDE)
    def _(n):
        i, t = n // (2 * SEQ // WIDE), lax.rem(n, 2 * SEQ // WIDE)
        attend(i, t * (WIDE // 2), WIDE, far_keys, 1, early)

    arrived(2)
    arrived(3)

    @pl.loop(0, 4 * SEQ // SIDE)
    def _(n):
        i, t = n // (2 * SEQ // SIDE), lax.rem(n, 2 * SEQ // SIDE)
        items, accs = attend(i, t * (SIDE // 2), SIDE, far_keys, 1, late)
        low = low_lanes((BLK, 128))
        for u in range(SIDE // 2):
            s = items[2 * u][0]
            left, right = accs[2 * u : 2 * u + 2]
            lsw, rsw = swap_halves(left), swap_halves(right)
            value = jnp.where(low, lsw, right)
            total = jnp.where(low, left, rsw)
            outs[i, s] = (value / total).astype(BF16)

        for u in range(SIDE // 2):
            d = t * (SIDE // 2) + u

            @pl.when(d > 0)
            def _(d=d):
                ret_copy(i, lax.rem(me + d, SEQ), d).start()

    for i in range(2):
        ret_own(i).start()

    @pl.loop(1, SEQ)
    def _(d):
        kv_copy(3, d).wait_send()

    wo_copy.wait()
    for i in range(2):
        ret_own(i).wait()

        @pl.loop(1, SEQ)
        def _(d, i=i):
            ret_copy(i, lax.rem(me + d, SEQ), d).wait()

        for g in range(HEADS // 2):
            a = ret[i, 2 * g].astype(F32)
            b = ret[i, 2 * g + 1].astype(F32)
            low = low_lanes(a.shape)
            col = slice(g * 128, (g + 1) * 128)
            att[:BLK, col] = jnp.where(low, a, swap_halves(b)).astype(BF16)
            att[BLK:, col] = jnp.where(low, swap_halves(a), b).astype(BF16)
        out = jnp.dot(att[...], wo_v[...], preferred_element_type=F32).astype(BF16)
        o_ref[i] = out[:BLK]
        o_ref[2 + i] = out[BLK:]


def write_out(x_ref, o_ref, sem):
    copies = [pltpu.make_async_copy(x_ref.at[b], o_ref.at[b], sem.at[b]) for b in range(OWN)]
    for copy in copies:
        copy.start()
    for copy in copies:
        copy.wait()


def on_device(nodes, w_qkv, w_out, kv_ids, counts):
    vm = pl.BlockSpec(memory_space=pltpu.VMEM)
    sm = pl.BlockSpec(memory_space=pltpu.SMEM)
    hbm = pl.BlockSpec(memory_space=pl.ANY)
    dma = pltpu.SemaphoreType.DMA
    out = pl.pallas_call(
        body,
        out_shape=pltpu.VMEM((OWN, BLK, D), BF16),
        in_specs=[sm, sm, hbm, hbm, hbm, hbm],
        out_specs=vm,
        scratch_shapes=[
            *[pltpu.VMEM((HEADS, OWN, r, 128), BF16) for r in ROWS],
            *[pltpu.VMEM((QB, r, 128), BF16) for r in ROWS],
            *[pltpu.VMEM((CL, REQ, r, 128), BF16) for r in ROWS],
            *[pltpu.VMEM((CL * REQ, r, 128), BF16) for r in ROWS],
            pltpu.VMEM((GROUPS, D, WCOL), BF16),
            pltpu.VMEM((D, D), BF16),
            pltpu.VMEM((HEADS, 2, BLK, 128), BF16),
            pltpu.VMEM((2, SEQ, BLK, 128), BF16),
            pltpu.VMEM((CL, 1, 128), jnp.int32),
            pltpu.VMEM((CL, 1, 128), jnp.int32),
            pltpu.SMEM((CL, 1, 128), jnp.int32),
            pltpu.VMEM((QB, 128), jnp.int32),
            pltpu.SMEM((QB, 128), jnp.int32),
            pltpu.VMEM((WIDE, NEAR // 4, BLK, 2 * BLK), F32),
            pltpu.VMEM((2, SEQ, 2, BLK, 128), F32),
            pltpu.VMEM((2, SEQ, 2, BLK, 128), F32),
            pltpu.VMEM((2, SEQ, BLK, 128), BF16),
            pltpu.VMEM((2, SEQ, BLK, 128), BF16),
            pltpu.VMEM((2 * BLK, D), BF16),
            pltpu.VMEM((128, 128), F32),
            pltpu.VMEM((OWN * BLK, D), BF16),
            pltpu.VMEM((KVB, QB), jnp.int32),
            dma((GROUPS + 1,)),
            dma((CL,)),
            dma((CL,)),
            dma((CH, SEQ)),
            dma((CH, SEQ)),
            dma((2, SEQ)),
            dma((2, SEQ)),
            dma((CH, CL)),
            dma((CH, CL)),
            dma((2, SEQ)),
            dma((2, SEQ)),
            dma((CH + 4,)),
            dma((4,)),
        ],
        compiler_params=pltpu.CompilerParams(
            collective_id=0, has_side_effects=True, vmem_limit_bytes=60 << 20
        ),
        name="sublayer",
    )(kv_ids.T, counts, nodes, kv_ids.T, w_qkv, w_out)
    return pl.pallas_call(
        write_out,
        out_shape=jax.ShapeDtypeStruct((OWN, BLK, D), BF16),
        in_specs=[vm],
        out_specs=hbm,
        scratch_shapes=[dma((OWN,))],
        compiler_params=pltpu.CompilerParams(vmem_limit_bytes=1 << 20),
        name="write_out",
    )(out).reshape(OWN * BLK, D)


def solution(mesh):
    placed = (P(("cluster", "seq"), None), P(), P(), P("cluster", None), P("cluster"))
    return jax.shard_map(
        on_device,
        mesh=mesh,
        in_specs=placed,
        out_specs=P(("cluster", "seq"), None),
        check_vma=False,
    )
```

```python
import functools

import jax
import jax.numpy as jnp
from jax import lax
from jax.experimental import pallas as pl
from jax.experimental.pallas import tpu as pltpu
from jax.sharding import PartitionSpec as P

D = 1024
HEADS = 16
HD = 64
BLK = 128
KVB = 16
REMOTE = 4
NEAR = KVB - REMOTE
QB = 64
REQ = 16
CL = 8
SEQ = 16
OWN = 4
ROWS = (32, 32, 32, 32)
CH = len(ROWS)
FIRST = tuple(sum(ROWS[:c]) for c in range(CH))
GROUPS = 4
WCOL = 3 * D // GROUPS
SIDE = 8
WIDE = 16
MESH = pl.DeviceIdType.MESH
F32 = jnp.float32
BF16 = jnp.bfloat16


def low_lanes(shape):
    return lax.broadcasted_iota(jnp.int32, shape, len(shape) - 1) < HD


def swap_halves(x):
    return pltpu.roll(x, HD, x.ndim - 1)


def body(ids_s, cnt_s, nodes_hbm, ids_hbm, w_hbm, wo_hbm, o_ref, *scratch):
    me = lax.axis_index("seq")
    mc = lax.axis_index("cluster")
    scratch = list(scratch)

    def take(n):
        got = scratch[:n]
        del scratch[:n]
        return got

    kvs, kvc, snd, far = take(CH), take(CH), take(CH), take(CH)
    w_v, wo_v, qs, qr, lsend, lrecv, lsm, far_v, far_s, sc, acc_v, top_v, outs, ret, att, turn, nodes, ids_v = take(18)
    w_sem, l_ss, l_rs, kv_ss, kv_rs, q_ss, q_rs, z_ss, z_rs, r_ss, r_rs, own_sem, sm_sem = scratch

    barrier = pltpu.get_barrier_semaphore()

    for d in range(1, SEQ):
        pl.semaphore_signal(barrier, inc=1, device_id={"seq": lax.rem(me + d, SEQ)}, device_id_type=MESH)
    for d in range(1, CL):
        pl.semaphore_signal(barrier, inc=1, device_id={"cluster": lax.rem(mc + d, CL)}, device_id_type=MESH)

    ids_copy = pltpu.make_async_copy(ids_hbm, ids_v, sm_sem.at[2])
    ids_copy.start()
    nodes_copy = pltpu.make_async_copy(nodes_hbm, nodes, sm_sem.at[3])
    nodes_copy.start()

    def w_copy(k):
        g = lax.rem(me // GROUPS + k, GROUPS)
        return pltpu.make_async_copy(
            w_hbm.at[:, pl.ds(pl.multiple_of(g * WCOL, 128), WCOL)], w_v.at[k], w_sem.at[k]
        )

    @pl.loop(0, GROUPS)
    def _(k):
        w_copy(k).start()

    wo_copy = pltpu.make_async_copy(wo_hbm, wo_v, w_sem.at[GROUPS])
    def kv_copy(c, d):
        peer = lax.rem(me + d, SEQ)
        return pltpu.make_async_remote_copy(
            src_ref=kvs[c].at[peer],
            dst_ref=kvc[c].at[pl.ds(OWN * me, OWN)],
            send_sem=kv_ss.at[c, d],
            recv_sem=kv_rs.at[c, d],
            device_id={"seq": peer},
            device_id_type=MESH,
        )

    def kv_own(c):
        return pltpu.make_async_copy(kvs[c].at[me], kvc[c].at[pl.ds(OWN * me, OWN)], own_sem.at[c])

    def q_copy(i, d):
        peer = lax.rem(me + d, SEQ)
        return pltpu.make_async_remote_copy(
            src_ref=qs.at[peer, i],
            dst_ref=qr.at[i, me],
            send_sem=q_ss.at[i, d],
            recv_sem=q_rs.at[i, d],
            device_id={"seq": peer},
            device_id_type=MESH,
        )

    def q_own(i):
        return pltpu.make_async_copy(qs.at[me, i], qr.at[i, me], own_sem.at[CH + i])

    def list_copy(d):
        peer = lax.rem(mc + d, CL)
        return pltpu.make_async_remote_copy(
            src_ref=lsend.at[peer],
            dst_ref=lrecv.at[CL - d],
            send_sem=l_ss.at[d],
            recv_sem=l_rs.at[d],
            device_id={"cluster": peer},
            device_id_type=MESH,
        )

    def z_copy(c, d):
        return pltpu.make_async_remote_copy(
            src_ref=snd[c].at[d],
            dst_ref=far[c].at[pl.ds(REQ * mc, REQ)],
            send_sem=z_ss.at[c, d],
            recv_sem=z_rs.at[c, d],
            device_id={"cluster": lax.rem(mc + d, CL)},
            device_id_type=MESH,
        )

    def ret_copy(i, peer, d):
        return pltpu.make_async_remote_copy(
            src_ref=outs.at[i, peer],
            dst_ref=ret.at[i, me],
            send_sem=r_ss.at[i, d],
            recv_sem=r_rs.at[i, d],
            device_id={"seq": peer},
            device_id_type=MESH,
        )

    def ret_own(i):
        return pltpu.make_async_copy(outs.at[i, me], ret.at[i, me], own_sem.at[CH + 2 + i])

    def start(own, copy):
        own.start()

        @pl.loop(1, SEQ)
        def _(d):
            copy(d).start()

    def start_after(done, own, copy):
        own.start()

        @pl.loop(1, SEQ)
        def _(d):
            done(d).wait_send()
            copy(d).start()

    def landed(own, copy):
        own.wait()

        @pl.loop(1, SEQ)
        def _(d):
            copy(d).wait_recv()

    def kv(c):
        return functools.partial(kv_copy, c)

    def qq(i):
        return functools.partial(q_copy, i)

    def pack(c):
        @pl.loop(1, CL)
        def _(d):
            for r in range(REQ):
                snd[c][d, r] = kvc[c][lsm[d, 0, r] & (QB - 1)]
            z_copy(c, d).start()

    turn[...] = jnp.zeros((128, 128), F32)
    ids_copy.wait()
    turn[:KVB, :QB] = ids_v[...].astype(F32)
    ids_t = jnp.transpose(turn[...])
    lane = lax.broadcasted_iota(jnp.int32, (QB, CL * QB), 1).astype(F32)
    hits = [ids_t[:QB, NEAR + j : NEAR + j + 1] == lane for j in range(REMOTE)]
    named = jnp.where(hits[0] | hits[1] | hits[2] | hits[3], 1.0, 0.0)
    present = jnp.max(named, axis=0, keepdims=True)
    present = jnp.broadcast_to(present, (8, CL * QB))
    lane8 = lax.broadcasted_iota(jnp.int32, (8, CL * QB), 1)
    inner = lane8 % QB
    rank = present
    step = 1
    while step < QB:
        rank = rank + jnp.where(inner >= step, pltpu.roll(rank, step, 1), 0.0)
        step *= 2
    rank = rank - present
    slot = lax.broadcasted_iota(jnp.int32, (REQ, CL * QB), 0).astype(F32)
    wanted = jnp.where((slot == rank[:1]) & (present[:1] > 0.5), 1.0, 0.0).astype(BF16)
    sub8 = lax.broadcasted_iota(jnp.int32, (CL, CL * QB), 0)
    worth = jnp.where(lane8 // QB == sub8, inner, 0).astype(F32).astype(BF16)
    wanted = jnp.concatenate([wanted, jnp.zeros((128 - REQ, CL * QB), BF16)], axis=0)
    lists = lax.dot_general(
        worth, wanted, (((1,), (1,)), ((), ())), preferred_element_type=F32
    ).astype(jnp.int32)
    for p in range(CL):
        lsend[p] = lists[p : p + 1]
    place = rank + (lane8 // QB * REQ).astype(F32)
    lane_q = lax.broadcasted_iota(jnp.int32, (QB, 128), 1)
    table = jnp.zeros((QB, 128), F32)
    for j in range(REMOTE):
        at = jnp.sum(jnp.where(hits[j], place[:1], 0.0), axis=1, keepdims=True)
        table = jnp.where(lane_q == j, at, table)
    far_v[...] = table.astype(jnp.int32)
    far_copy = pltpu.make_async_copy(far_v, far_s, sm_sem.at[1])
    far_copy.start()

    def project(k, x):
        p = jnp.dot(x, w_v[k], preferred_element_type=F32)
        return [[p[:, 384 * n + 128 * e : 384 * n + 128 * e + 128] for e in range(3)] for n in range(2)]

    def group(k):
        return lax.rem(me // GROUPS + k, GROUPS)

    nodes_copy.wait()
    x0 = jnp.concatenate([nodes[b * BLK : b * BLK + ROWS[0]] for b in range(OWN)], axis=0)

    @pl.loop(0, GROUPS)
    def _(k):
        w_copy(k).wait()
        low = low_lanes((OWN * ROWS[0], 128))
        for n, (t0, t1, t2) in enumerate(project(k, x0)):
            h0 = 4 * group(k) + 2 * n
            kv0 = jnp.where(low, swap_halves(t0), swap_halves(t1))
            kvs[0][h0] = kv0.astype(BF16).reshape(OWN, ROWS[0], 128)
            kvs[0][h0 + 1] = t2.astype(BF16).reshape(OWN, ROWS[0], 128)

    pl.semaphore_wait(barrier, SEQ + CL - 2)
    for d in range(1, CL):
        list_copy(d).start()
    for d in range(1, SEQ):
        kv_copy(0, d).start()
    kv_own(0).start()
    wo_copy.start()

    @pl.loop(0, GROUPS)
    def _(k):
        low = low_lanes((OWN * BLK, 128))
        half = OWN * BLK // 2
        scale = HD**-0.5
        for n, (t0, t1, t2) in enumerate(project(k, nodes[...])):
            r0, r1 = swap_halves(t0), swap_halves(t1)
            h0 = 4 * group(k) + 2 * n
            kv0 = jnp.where(low, r0, r1).astype(BF16).reshape(OWN, BLK, 128)
            kv1 = t2.astype(BF16).reshape(OWN, BLK, 128)
            for c in range(1, CH):
                kvs[c][h0] = kv0[:, FIRST[c] : FIRST[c] + ROWS[c]]
                kvs[c][h0 + 1] = kv1[:, FIRST[c] : FIRST[c] + ROWS[c]]
            q0 = jnp.where(low[:half], t0[:half], r0[half:]) * scale
            q1 = jnp.where(low[:half], r1[:half], t1[half:]) * scale
            qs[h0] = q0.astype(BF16).reshape(2, BLK, 128)
            qs[h0 + 1] = q1.astype(BF16).reshape(2, BLK, 128)

    start_after(kv(0), kv_own(1), kv(1))
    @pl.loop(1, CL)
    def _(d):
        list_copy(d).wait()

    sm_copy = pltpu.make_async_copy(
        lrecv.at[pl.ds(1, CL - 1)], lsm.at[pl.ds(1, CL - 1)], sm_sem.at[0]
    )
    sm_copy.start()
    sm_copy.wait()

    def near_keys(qb, pieces):
        return jnp.concatenate([kvc[c][ids_s[j, qb] & (QB - 1)] for c, j in pieces], axis=0)

    def far_keys(qb, pieces):
        return jnp.concatenate([far[c][far_s[qb, j] & (CL * REQ - 1)] for c, j in pieces], axis=0)

    def tiles_of(slots, chunks):
        pieces = [(c, j) for c in chunks for j in range(slots)]
        per = 2 * BLK // ROWS[0]
        return [pieces[n : n + per] for n in range(0, len(pieces), per)]

    def score(q, kv):
        return lax.dot_general(q, kv, (((1,), (1,)), ((), ())), preferred_element_type=F32)

    def weigh(s, m, kv):
        p = jnp.exp(s - m).astype(BF16)
        v1 = jnp.where(low_lanes(kv.shape), jnp.ones_like(kv), kv)
        return jnp.dot(p, v1, preferred_element_type=F32)

    def queries(i, s):
        qp = qr[i, s]
        low = low_lanes(qp.shape)
        left = jnp.where(low, qp, jnp.zeros_like(qp))
        right = jnp.where(low, swap_halves(qp.astype(F32)), 0.0).astype(BF16)
        return left, right

    def items_of(i, first, count):
        items = []
        for u in range(count // 2):
            s = lax.rem(me + first + u, SEQ)
            for half, q in enumerate(queries(i, s)):
                items.append((s, half, q, s * OWN + i + 2 * half))
        return items

    def attend(i, begin, count, keys, chunks):
        remote, first = keys is far_keys, keys is near_keys and chunks[0] == 0
        items = items_of(i, begin, count)
        tiles = tiles_of(REMOTE if remote else NEAR, chunks)
        tops, accs = [None] * count, [None] * count
        for jj, tile in enumerate(tiles):
            for g, (s, half, q, qb) in enumerate(items):
                sco = score(q, keys(qb, tile))
                if remote:
                    slot = lax.broadcasted_iota(jnp.int32, sco.shape, 1) // ROWS[0] % REMOTE
                    sco = jnp.where(slot < cnt_s[qb] - NEAR, sco, -1e30)
                sc[g, jj, :, : sco.shape[1]] = sco
                top = sco if sco.shape[1] == BLK else jnp.maximum(sco[:, :BLK], sco[:, BLK:])
                tops[g] = top if jj == 0 else jnp.maximum(tops[g], top)
        for g, (s, half, q, qb) in enumerate(items):
            top = tops[g] if first else jnp.maximum(tops[g], top_v[i, s, half])
            tops[g] = jnp.max(top, axis=1, keepdims=True)
        for jj, tile in enumerate(tiles):
            for g, (s, half, q, qb) in enumerate(items):
                kv = keys(qb, tile)
                a = weigh(sc[g, jj, :, : kv.shape[0]], tops[g], kv)
                accs[g] = a if jj == 0 else accs[g] + a
        for g, (s, half, q, qb) in enumerate(items):
            if not first:
                accs[g] = accs[g] + acc_v[i, s, half] * jnp.exp(top_v[i, s, half] - tops[g])
            if not (remote and chunks[-1] == CH - 1):
                acc_v[i, s, half] = accs[g]
                top_v[i, s, half] = jnp.broadcast_to(tops[g], (BLK, 128))
        return items, accs

    early, late = (0, 1, 2), (3,)

    def near(i, chunks):
        @pl.loop(0, 2 * SEQ // WIDE)
        def _(t):
            attend(i, t * (WIDE // 2), WIDE, near_keys, chunks)

    for c in early:
        landed(kv_own(c), kv(c))
        pack(c)
        if c == 0:
            start_after(kv(1), kv_own(2), kv(2))
        elif c == 1:
            start_after(kv(2), q_own(0), qq(0))
    start_after(qq(0), q_own(1), qq(1))
    start(kv_own(3), kv(3))
    landed(q_own(0), qq(0))
    near(0, early)
    landed(q_own(1), qq(1))
    near(1, early)
    landed(kv_own(3), kv(3))
    pack(3)

    @pl.loop(0, 2)
    def _(i):
        near(i, late)

    far_copy.wait()

    def arrived(c):
        @pl.loop(1, CL)
        def _(d):
            z_copy(c, d).wait()

    for c in early:
        arrived(c)

    @pl.loop(0, 4 * SEQ // WIDE)
    def _(n):
        i, t = n // (2 * SEQ // WIDE), lax.rem(n, 2 * SEQ // WIDE)
        attend(i, t * (WIDE // 2), WIDE, far_keys, early)

    arrived(3)

    @pl.loop(0, 4 * SEQ // SIDE)
    def _(n):
        i, t = n // (2 * SEQ // SIDE), lax.rem(n, 2 * SEQ // SIDE)
        items, accs = attend(i, t * (SIDE // 2), SIDE, far_keys, late)
        low = low_lanes((BLK, 128))
        for u in range(SIDE // 2):
            s = items[2 * u][0]
            left, right = accs[2 * u : 2 * u + 2]
            lsw, rsw = swap_halves(left), swap_halves(right)
            value = jnp.where(low, lsw, right)
            total = jnp.where(low, left, rsw)
            outs[i, s] = (value / total).astype(BF16)

        for u in range(SIDE // 2):
            d = t * (SIDE // 2) + u

            @pl.when(d > 0)
            def _(d=d):
                ret_copy(i, lax.rem(me + d, SEQ), d).start()

    for i in range(2):
        ret_own(i).start()

    @pl.loop(1, SEQ)
    def _(d):
        q_copy(1, d).wait_send()
        kv_copy(3, d).wait_send()

    wo_copy.wait()
    for i in range(2):
        ret_own(i).wait()

        @pl.loop(1, SEQ)
        def _(d, i=i):
            ret_copy(i, lax.rem(me + d, SEQ), d).wait()

        for g in range(HEADS // 2):
            a = ret[i, 2 * g].astype(F32)
            b = ret[i, 2 * g + 1].astype(F32)
            low = low_lanes(a.shape)
            col = slice(g * 128, (g + 1) * 128)
            att[:BLK, col] = jnp.where(low, a, swap_halves(b)).astype(BF16)
            att[BLK:, col] = jnp.where(low, swap_halves(a), b).astype(BF16)
        out = jnp.dot(att[...], wo_v[...], preferred_element_type=F32).astype(BF16)
        o_ref[i] = out[:BLK]
        o_ref[2 + i] = out[BLK:]


def write_out(x_ref, o_ref, sem):
    copies = [pltpu.make_async_copy(x_ref.at[b], o_ref.at[b], sem.at[b]) for b in range(OWN)]
    for copy in copies:
        copy.start()
    for copy in copies:
        copy.wait()


def on_device(nodes, w_qkv, w_out, kv_ids, counts):
    vm = pl.BlockSpec(memory_space=pltpu.VMEM)
    sm = pl.BlockSpec(memory_space=pltpu.SMEM)
    hbm = pl.BlockSpec(memory_space=pl.ANY)
    dma = pltpu.SemaphoreType.DMA
    out = pl.pallas_call(
        body,
        out_shape=pltpu.VMEM((OWN, BLK, D), BF16),
        in_specs=[sm, sm, hbm, hbm, hbm, hbm],
        out_specs=vm,
        scratch_shapes=[
            *[pltpu.VMEM((HEADS, OWN, r, 128), BF16) for r in ROWS],
            *[pltpu.VMEM((QB, r, 128), BF16) for r in ROWS],
            *[pltpu.VMEM((CL, REQ, r, 128), BF16) for r in ROWS],
            *[pltpu.VMEM((CL * REQ, r, 128), BF16) for r in ROWS],
            pltpu.VMEM((GROUPS, D, WCOL), BF16),
            pltpu.VMEM((D, D), BF16),
            pltpu.VMEM((HEADS, 2, BLK, 128), BF16),
            pltpu.VMEM((2, SEQ, BLK, 128), BF16),
            pltpu.VMEM((CL, 1, 128), jnp.int32),
            pltpu.VMEM((CL, 1, 128), jnp.int32),
            pltpu.SMEM((CL, 1, 128), jnp.int32),
            pltpu.VMEM((QB, 128), jnp.int32),
            pltpu.SMEM((QB, 128), jnp.int32),
            pltpu.VMEM((WIDE, 5, BLK, 2 * BLK), F32),
            pltpu.VMEM((2, SEQ, 2, BLK, 128), F32),
            pltpu.VMEM((2, SEQ, 2, BLK, 128), F32),
            pltpu.VMEM((2, SEQ, BLK, 128), BF16),
            pltpu.VMEM((2, SEQ, BLK, 128), BF16),
            pltpu.VMEM((2 * BLK, D), BF16),
            pltpu.VMEM((128, 128), F32),
            pltpu.VMEM((OWN * BLK, D), BF16),
            pltpu.VMEM((KVB, QB), jnp.int32),
            dma((GROUPS + 1,)),
            dma((CL,)),
            dma((CL,)),
            dma((CH, SEQ)),
            dma((CH, SEQ)),
            dma((2, SEQ)),
            dma((2, SEQ)),
            dma((CH, CL)),
            dma((CH, CL)),
            dma((2, SEQ)),
            dma((2, SEQ)),
            dma((CH + 4,)),
            dma((4,)),
        ],
        compiler_params=pltpu.CompilerParams(
            collective_id=0, has_side_effects=True, vmem_limit_bytes=60 << 20
        ),
        name="sublayer",
    )(kv_ids.T, counts, nodes, kv_ids.T, w_qkv, w_out)
    return pl.pallas_call(
        write_out,
        out_shape=jax.ShapeDtypeStruct((OWN, BLK, D), BF16),
        in_specs=[vm],
        out_specs=hbm,
        scratch_shapes=[dma((OWN,))],
        compiler_params=pltpu.CompilerParams(vmem_limit_bytes=1 << 20),
        name="write_out",
    )(out).reshape(OWN * BLK, D)


def solution(mesh):
    placed = (P(("cluster", "seq"), None), P(), P(), P("cluster", None), P("cluster"))
    return jax.shard_map(
        on_device,
        mesh=mesh,
        in_specs=placed,
        out_specs=P(("cluster", "seq"), None),
        check_vma=False,
    )
```

```python
import functools

import jax
import jax.numpy as jnp
from jax import lax
from jax.experimental import pallas as pl
from jax.experimental.pallas import tpu as pltpu
from jax.sharding import PartitionSpec as P

D = 1024
HEADS = 16
HD = 64
BLK = 128
KVB = 16
REMOTE = 4
NEAR = KVB - REMOTE
LEAST = 13
QB = 64
REQ = 16
CL = 8
SEQ = 16
OWN = 4
ROWS = (16, 16, 32, 32, 32)
CH = len(ROWS)
FIRST = tuple(sum(ROWS[:c]) for c in range(CH))
GROUPS = 4
WCOL = 3 * D // GROUPS
SIDE = 8
WIDE = 16
MESH = pl.DeviceIdType.MESH
F32 = jnp.float32
BF16 = jnp.bfloat16


def low_lanes(shape):
    return lax.broadcasted_iota(jnp.int32, shape, len(shape) - 1) < HD


def swap_halves(x):
    return pltpu.roll(x, HD, x.ndim - 1)


def body(ids_s, cnt_s, nodes_hbm, ids_hbm, w_hbm, wo_hbm, o_ref, *scratch):
    me = lax.axis_index("seq")
    mc = lax.axis_index("cluster")
    scratch = list(scratch)

    def take(n):
        got = scratch[:n]
        del scratch[:n]
        return got

    kvs, kvc, snd, far = take(CH), take(CH), take(CH), take(CH)
    w_v, wo_v, qs, qr, lsend, lrecv, lsm, far_v, far_s, sc, acc_v, top_v, outs, ret, att, turn, nodes, ids_v = take(18)
    w_sem, l_ss, l_rs, kv_ss, kv_rs, q_ss, q_rs, z_ss, z_rs, r_ss, r_rs, own_sem, sm_sem = scratch

    barrier = pltpu.get_barrier_semaphore()

    for d in range(1, SEQ):
        pl.semaphore_signal(barrier, inc=1, device_id={"seq": lax.rem(me + d, SEQ)}, device_id_type=MESH)
    for d in range(1, CL):
        pl.semaphore_signal(barrier, inc=1, device_id={"cluster": lax.rem(mc + d, CL)}, device_id_type=MESH)

    ids_copy = pltpu.make_async_copy(ids_hbm, ids_v, sm_sem.at[2])
    ids_copy.start()
    nodes_copy = pltpu.make_async_copy(nodes_hbm, nodes, sm_sem.at[3])
    nodes_copy.start()

    def w_copy(k):
        g = lax.rem(me // GROUPS + k, GROUPS)
        return pltpu.make_async_copy(
            w_hbm.at[:, pl.ds(pl.multiple_of(g * WCOL, 128), WCOL)], w_v.at[k], w_sem.at[k]
        )

    @pl.loop(0, GROUPS)
    def _(k):
        w_copy(k).start()

    wo_copy = pltpu.make_async_copy(wo_hbm, wo_v, w_sem.at[GROUPS])
    def kv_copy(c, d):
        peer = lax.rem(me + d, SEQ)
        return pltpu.make_async_remote_copy(
            src_ref=kvs[c].at[peer],
            dst_ref=kvc[c].at[pl.ds(OWN * me, OWN)],
            send_sem=kv_ss.at[c, d],
            recv_sem=kv_rs.at[c, d],
            device_id={"seq": peer},
            device_id_type=MESH,
        )

    def kv_own(c):
        return pltpu.make_async_copy(kvs[c].at[me], kvc[c].at[pl.ds(OWN * me, OWN)], own_sem.at[c])

    def q_copy(i, d):
        peer = lax.rem(me + d, SEQ)
        return pltpu.make_async_remote_copy(
            src_ref=qs.at[peer, i],
            dst_ref=qr.at[i, me],
            send_sem=q_ss.at[i, d],
            recv_sem=q_rs.at[i, d],
            device_id={"seq": peer},
            device_id_type=MESH,
        )

    def q_own(i):
        return pltpu.make_async_copy(qs.at[me, i], qr.at[i, me], own_sem.at[CH + i])

    def list_copy(d):
        peer = lax.rem(mc + d, CL)
        return pltpu.make_async_remote_copy(
            src_ref=lsend.at[peer],
            dst_ref=lrecv.at[CL - d],
            send_sem=l_ss.at[d],
            recv_sem=l_rs.at[d],
            device_id={"cluster": peer},
            device_id_type=MESH,
        )

    def z_copy(c, d):
        return pltpu.make_async_remote_copy(
            src_ref=snd[c].at[d],
            dst_ref=far[c].at[pl.ds(REQ * mc, REQ)],
            send_sem=z_ss.at[c, d],
            recv_sem=z_rs.at[c, d],
            device_id={"cluster": lax.rem(mc + d, CL)},
            device_id_type=MESH,
        )

    def ret_copy(i, peer, d):
        return pltpu.make_async_remote_copy(
            src_ref=outs.at[i, peer],
            dst_ref=ret.at[i, me],
            send_sem=r_ss.at[i, d],
            recv_sem=r_rs.at[i, d],
            device_id={"seq": peer},
            device_id_type=MESH,
        )

    def ret_own(i):
        return pltpu.make_async_copy(outs.at[i, me], ret.at[i, me], own_sem.at[CH + 2 + i])

    def start(own, copy):
        own.start()

        @pl.loop(1, SEQ)
        def _(d):
            copy(d).start()

    def start_after(done, own, copy):
        own.start()

        @pl.loop(1, SEQ)
        def _(d):
            done(d).wait_send()
            copy(d).start()

    def landed(own, copy):
        own.wait()

        @pl.loop(1, SEQ)
        def _(d):
            copy(d).wait_recv()

    def kv(c):
        return functools.partial(kv_copy, c)

    def qq(i):
        return functools.partial(q_copy, i)

    def pack(c):
        @pl.loop(1, CL)
        def _(d):
            for r in range(REQ):
                snd[c][d, r] = kvc[c][lsm[d, 0, r] & (QB - 1)]
            z_copy(c, d).start()

    turn[...] = jnp.zeros((128, 128), F32)
    ids_copy.wait()
    turn[:KVB, :QB] = ids_v[...].astype(F32)
    ids_t = jnp.transpose(turn[...])
    lane = lax.broadcasted_iota(jnp.int32, (QB, CL * QB), 1).astype(F32)
    hits = [ids_t[:QB, NEAR + j : NEAR + j + 1] == lane for j in range(REMOTE)]
    named = jnp.where(hits[0] | hits[1] | hits[2] | hits[3], 1.0, 0.0)
    present = jnp.max(named, axis=0, keepdims=True)
    present = jnp.broadcast_to(present, (8, CL * QB))
    lane8 = lax.broadcasted_iota(jnp.int32, (8, CL * QB), 1)
    inner = lane8 % QB
    rank = present
    step = 1
    while step < QB:
        rank = rank + jnp.where(inner >= step, pltpu.roll(rank, step, 1), 0.0)
        step *= 2
    rank = rank - present
    slot = lax.broadcasted_iota(jnp.int32, (REQ, CL * QB), 0).astype(F32)
    wanted = jnp.where((slot == rank[:1]) & (present[:1] > 0.5), 1.0, 0.0).astype(BF16)
    sub8 = lax.broadcasted_iota(jnp.int32, (CL, CL * QB), 0)
    worth = jnp.where(lane8 // QB == sub8, inner, 0).astype(F32).astype(BF16)
    wanted = jnp.concatenate([wanted, jnp.zeros((128 - REQ, CL * QB), BF16)], axis=0)
    lists = lax.dot_general(
        worth, wanted, (((1,), (1,)), ((), ())), preferred_element_type=F32
    ).astype(jnp.int32)
    for p in range(CL):
        lsend[p] = lists[p : p + 1]
    place = rank + (lane8 // QB * REQ).astype(F32)
    lane_q = lax.broadcasted_iota(jnp.int32, (QB, 128), 1)
    table = jnp.zeros((QB, 128), F32)
    for j in range(REMOTE):
        at = jnp.sum(jnp.where(hits[j], place[:1], 0.0), axis=1, keepdims=True)
        table = jnp.where(lane_q == j, at, table)
    far_v[...] = table.astype(jnp.int32)
    far_copy = pltpu.make_async_copy(far_v, far_s, sm_sem.at[1])
    far_copy.start()

    def project(k, x):
        p = jnp.dot(x, w_v[k], preferred_element_type=F32)
        return [[p[:, 384 * n + 128 * e : 384 * n + 128 * e + 128] for e in range(3)] for n in range(2)]

    def group(k):
        return lax.rem(me // GROUPS + k, GROUPS)

    def send_group(c, k):
        @pl.loop(0, HEADS // GROUPS)
        def _(h):
            d = lax.rem(group(k) * (HEADS // GROUPS) + h + SEQ - me, SEQ)

            @pl.when(d > 0)
            def _():
                kv_copy(c, d).start()

    nodes_copy.wait()
    x0 = jnp.concatenate([nodes[b * BLK : b * BLK + ROWS[0]] for b in range(OWN)], axis=0)

    @pl.loop(0, GROUPS)
    def _(k):
        w_copy(k).wait()
        low = low_lanes((OWN * ROWS[0], 128))
        for n, (t0, t1, t2) in enumerate(project(k, x0)):
            h0 = 4 * group(k) + 2 * n
            kv0 = jnp.where(low, swap_halves(t0), swap_halves(t1))
            kvs[0][h0] = kv0.astype(BF16).reshape(OWN, ROWS[0], 128)
            kvs[0][h0 + 1] = t2.astype(BF16).reshape(OWN, ROWS[0], 128)

        @pl.when(k == 0)
        def _():
            pl.semaphore_wait(barrier, SEQ + CL - 2)

            @pl.loop(1, CL)
            def _(d):
                list_copy(d).start()

        send_group(0, k)

    kv_own(0).start()
    wo_copy.start()

    @pl.loop(0, GROUPS)
    def _(k):
        @pl.when(k == GROUPS // 2)
        def _():
            @pl.loop(1, CL)
            def _(d):
                list_copy(d).wait()

            sm_copy = pltpu.make_async_copy(
                lrecv.at[pl.ds(1, CL - 1)], lsm.at[pl.ds(1, CL - 1)], sm_sem.at[0]
            )
            sm_copy.start()
            sm_copy.wait()


            landed(kv_own(0), kv(0))
            pack(0)

        low = low_lanes((OWN * BLK, 128))
        half = OWN * BLK // 2
        scale = HD**-0.5
        for n, (t0, t1, t2) in enumerate(project(k, nodes[...])):
            r0, r1 = swap_halves(t0), swap_halves(t1)
            h0 = 4 * group(k) + 2 * n
            kv0 = jnp.where(low, r0, r1).astype(BF16).reshape(OWN, BLK, 128)
            kv1 = t2.astype(BF16).reshape(OWN, BLK, 128)
            for c in range(1, CH):
                kvs[c][h0] = kv0[:, FIRST[c] : FIRST[c] + ROWS[c]]
                kvs[c][h0 + 1] = kv1[:, FIRST[c] : FIRST[c] + ROWS[c]]
            q0 = jnp.where(low[:half], t0[:half], r0[half:]) * scale
            q1 = jnp.where(low[:half], r1[:half], t1[half:]) * scale
            qs[h0] = q0.astype(BF16).reshape(2, BLK, 128)
            qs[h0 + 1] = q1.astype(BF16).reshape(2, BLK, 128)
        send_group(1, k)

    kv_own(1).start()
    start_after(kv(1), kv_own(2), kv(2))
    for c in range(1, CH):
        landed(kv_own(c), kv(c))
        pack(c)
        if c + 2 < CH:
            start_after(kv(c + 1), kv_own(c + 2), kv(c + 2))
        elif c + 2 == CH:
            start_after(kv(c + 1), q_own(0), qq(0))
    start_after(qq(0), q_own(1), qq(1))

    def block_of(bufs, b):
        return [bufs[c][b] for c in range(CH)]

    def pair_of(bufs, b0, b1):
        return jnp.concatenate(block_of(bufs, b0) + block_of(bufs, b1), axis=0)

    def near_pair(qb, j):
        return pair_of(kvc, ids_s[j, qb] & (QB - 1), ids_s[j + 1, qb] & (QB - 1))

    def far_pair(qb, j):
        last = CL * REQ - 1
        return pair_of(far, far_s[qb, j] & last, far_s[qb, j + 1] & last)

    def score(q, kv):
        return lax.dot_general(q, kv, (((1,), (1,)), ((), ())), preferred_element_type=F32)

    def weigh(s, m, kv):
        p = jnp.exp(s - m).astype(BF16)
        v1 = jnp.where(low_lanes(kv.shape), jnp.ones_like(kv), kv)
        return jnp.dot(p, v1, preferred_element_type=F32)

    def queries(i, s):
        qp = qr[i, s]
        low = low_lanes(qp.shape)
        left = jnp.where(low, qp, jnp.zeros_like(qp))
        right = jnp.where(low, swap_halves(qp.astype(F32)), 0.0).astype(BF16)
        return left, right

    def items_of(i, first, count):
        items = []
        for u in range(count // 2):
            s = lax.rem(me + first + u, SEQ)
            for half, q in enumerate(queries(i, s)):
                items.append((s, half, q, s * OWN + i + 2 * half))
        return items

    def near(i):
        @pl.loop(0, 2 * SEQ // WIDE)
        def _(t):
            items = items_of(i, t * (WIDE // 2), WIDE)
            tops = [None] * WIDE
            for jj in range(NEAR // 2):
                for g, (s, half, q, qb) in enumerate(items):
                    sco = score(q, near_pair(qb, 2 * jj))
                    sc[g, jj] = sco
                    top = jnp.maximum(sco[:, :BLK], sco[:, BLK:])
                    tops[g] = top if jj == 0 else jnp.maximum(tops[g], top)
            tops = [jnp.max(top, axis=1, keepdims=True) for top in tops]
            accs = [None] * WIDE
            for jj in range(NEAR // 2):
                for g, (s, half, q, qb) in enumerate(items):
                    a = weigh(sc[g, jj], tops[g], near_pair(qb, 2 * jj))
                    accs[g] = a if jj == 0 else accs[g] + a
            for g, (s, half, q, qb) in enumerate(items):
                acc_v[i, s, half] = accs[g]
                top_v[i, s, half] = jnp.broadcast_to(tops[g], (BLK, 128))

    def distant(i):
        @pl.loop(0, 2 * SEQ // SIDE)
        def _(t):
            items = items_of(i, t * (SIDE // 2), SIDE)
            pairs = [[far_pair(qb, 2 * jj) for jj in range(REMOTE // 2)] for _, _, _, qb in items]
            scores, tops, accs = [], [], []
            for g, (s, half, q, qb) in enumerate(items):
                pieces = []
                for jj in range(REMOTE // 2):
                    sco = score(q, pairs[g][jj])
                    for part in range(2):
                        piece = sco[:, part * BLK : (part + 1) * BLK]
                        slot = NEAR + 2 * jj + part
                        if slot >= LEAST:
                            piece = jnp.where(slot < cnt_s[qb], piece, -1e30)
                        pieces.append(piece)
                scores.append(pieces)
            for g, (s, half, q, qb) in enumerate(items):
                m = top_v[i, s, half]
                for piece in scores[g]:
                    m = jnp.maximum(m, piece)
                tops.append(jnp.max(m, axis=1, keepdims=True))
            for g, (s, half, q, qb) in enumerate(items):
                acc = acc_v[i, s, half] * jnp.exp(top_v[i, s, half] - tops[g])
                for jj in range(REMOTE // 2):
                    both = jnp.concatenate(scores[g][2 * jj : 2 * jj + 2], axis=1)
                    acc = acc + weigh(both, tops[g], pairs[g][jj])
                accs.append(acc)
            low = low_lanes((BLK, 128))
            for u in range(SIDE // 2):
                s = items[2 * u][0]
                left, right = accs[2 * u : 2 * u + 2]
                lsw, rsw = swap_halves(left), swap_halves(right)
                value = jnp.where(low, lsw, right)
                total = jnp.where(low, left, rsw)
                outs[i, s] = (value / total).astype(BF16)

            for u in range(SIDE // 2):
                d = t * (SIDE // 2) + u

                @pl.when(d > 0)
                def _(d=d):
                    ret_copy(i, lax.rem(me + d, SEQ), d).start()

    landed(q_own(0), qq(0))
    near(0)
    landed(q_own(1), qq(1))
    near(1)

    for c in range(CH):

        @pl.loop(1, CL)
        def _(d, c=c):
            z_copy(c, d).wait()

    far_copy.wait()
    for i in range(2):
        distant(i)
        ret_own(i).start()

    @pl.loop(1, SEQ)
    def _(d):
        q_copy(1, d).wait_send()
        kv_copy(0, d).wait_send()

    wo_copy.wait()
    for i in range(2):
        ret_own(i).wait()

        @pl.loop(1, SEQ)
        def _(d, i=i):
            ret_copy(i, lax.rem(me + d, SEQ), d).wait()

        for g in range(HEADS // 2):
            a = ret[i, 2 * g].astype(F32)
            b = ret[i, 2 * g + 1].astype(F32)
            low = low_lanes(a.shape)
            col = slice(g * 128, (g + 1) * 128)
            att[:BLK, col] = jnp.where(low, a, swap_halves(b)).astype(BF16)
            att[BLK:, col] = jnp.where(low, swap_halves(a), b).astype(BF16)
        out = jnp.dot(att[...], wo_v[...], preferred_element_type=F32).astype(BF16)
        o_ref[i] = out[:BLK]
        o_ref[2 + i] = out[BLK:]


def write_out(x_ref, o_ref, sem):
    copies = [pltpu.make_async_copy(x_ref.at[b], o_ref.at[b], sem.at[b]) for b in range(OWN)]
    for copy in copies:
        copy.start()
    for copy in copies:
        copy.wait()


def on_device(nodes, w_qkv, w_out, kv_ids, counts):
    vm = pl.BlockSpec(memory_space=pltpu.VMEM)
    sm = pl.BlockSpec(memory_space=pltpu.SMEM)
    hbm = pl.BlockSpec(memory_space=pl.ANY)
    dma = pltpu.SemaphoreType.DMA
    out = pl.pallas_call(
        body,
        out_shape=pltpu.VMEM((OWN, BLK, D), BF16),
        in_specs=[sm, sm, hbm, hbm, hbm, hbm],
        out_specs=vm,
        scratch_shapes=[
            *[pltpu.VMEM((HEADS, OWN, r, 128), BF16) for r in ROWS],
            *[pltpu.VMEM((QB, r, 128), BF16) for r in ROWS],
            *[pltpu.VMEM((CL, REQ, r, 128), BF16) for r in ROWS],
            *[pltpu.VMEM((CL * REQ, r, 128), BF16) for r in ROWS],
            pltpu.VMEM((GROUPS, D, WCOL), BF16),
            pltpu.VMEM((D, D), BF16),
            pltpu.VMEM((HEADS, 2, BLK, 128), BF16),
            pltpu.VMEM((2, SEQ, BLK, 128), BF16),
            pltpu.VMEM((CL, 1, 128), jnp.int32),
            pltpu.VMEM((CL, 1, 128), jnp.int32),
            pltpu.SMEM((CL, 1, 128), jnp.int32),
            pltpu.VMEM((QB, 128), jnp.int32),
            pltpu.SMEM((QB, 128), jnp.int32),
            pltpu.VMEM((WIDE, NEAR // 2, BLK, 2 * BLK), F32),
            pltpu.VMEM((2, SEQ, 2, BLK, 128), F32),
            pltpu.VMEM((2, SEQ, 2, BLK, 128), F32),
            pltpu.VMEM((2, SEQ, BLK, 128), BF16),
            pltpu.VMEM((2, SEQ, BLK, 128), BF16),
            pltpu.VMEM((2 * BLK, D), BF16),
            pltpu.VMEM((128, 128), F32),
            pltpu.VMEM((OWN * BLK, D), BF16),
            pltpu.VMEM((KVB, QB), jnp.int32),
            dma((GROUPS + 1,)),
            dma((CL,)),
            dma((CL,)),
            dma((CH, SEQ)),
            dma((CH, SEQ)),
            dma((2, SEQ)),
            dma((2, SEQ)),
            dma((CH, CL)),
            dma((CH, CL)),
            dma((2, SEQ)),
            dma((2, SEQ)),
            dma((CH + 4,)),
            dma((4,)),
        ],
        compiler_params=pltpu.CompilerParams(
            collective_id=0, has_side_effects=True, vmem_limit_bytes=60 << 20
        ),
        name="sublayer",
    )(kv_ids.T, counts, nodes, kv_ids.T, w_qkv, w_out)
    return pl.pallas_call(
        write_out,
        out_shape=jax.ShapeDtypeStruct((OWN, BLK, D), BF16),
        in_specs=[vm],
        out_specs=hbm,
        scratch_shapes=[dma((OWN,))],
        compiler_params=pltpu.CompilerParams(vmem_limit_bytes=1 << 20),
        name="write_out",
    )(out).reshape(OWN * BLK, D)


def solution(mesh):
    placed = (P(("cluster", "seq"), None), P(), P(), P("cluster", None), P("cluster"))
    return jax.shard_map(
        on_device,
        mesh=mesh,
        in_specs=placed,
        out_specs=P(("cluster", "seq"), None),
        check_vma=False,
    )
```

```python
import functools

import jax
import jax.numpy as jnp
from jax import lax
from jax.experimental import pallas as pl
from jax.experimental.pallas import tpu as pltpu
from jax.sharding import PartitionSpec as P

D = 1024
HEADS = 16
HD = 64
BLK = 128
KVB = 16
REMOTE = 4
NEAR = KVB - REMOTE
LEAST = 13
QB = 64
REQ = 16
CL = 8
SEQ = 16
OWN = 4
ROWS = (16, 32, 32, 48)
CH = len(ROWS)
FIRST = tuple(sum(ROWS[:c]) for c in range(CH))
GROUPS = 4
WCOL = 3 * D // GROUPS
SIDE = 8
WIDE = 16
MESH = pl.DeviceIdType.MESH
F32 = jnp.float32
BF16 = jnp.bfloat16


def low_lanes(shape):
    return lax.broadcasted_iota(jnp.int32, shape, len(shape) - 1) < HD


def swap_halves(x):
    return pltpu.roll(x, HD, x.ndim - 1)


def body(ids_s, cnt_s, nodes_hbm, ids_hbm, w_hbm, wo_hbm, o_ref, *scratch):
    me = lax.axis_index("seq")
    mc = lax.axis_index("cluster")
    scratch = list(scratch)

    def take(n):
        got = scratch[:n]
        del scratch[:n]
        return got

    kvs, kvc, snd, far = take(CH), take(CH), take(CH), take(CH)
    w_v, wo_v, qs, qr, lsend, lrecv, lsm, far_v, far_s, sc, acc_v, top_v, outs, ret, att, turn, nodes, ids_v = take(18)
    w_sem, l_ss, l_rs, kv_ss, kv_rs, q_ss, q_rs, z_ss, z_rs, r_ss, r_rs, own_sem, sm_sem = scratch

    barrier = pltpu.get_barrier_semaphore()

    for d in range(1, SEQ):
        pl.semaphore_signal(barrier, inc=1, device_id={"seq": lax.rem(me + d, SEQ)}, device_id_type=MESH)
    for d in range(1, CL):
        pl.semaphore_signal(barrier, inc=1, device_id={"cluster": lax.rem(mc + d, CL)}, device_id_type=MESH)

    ids_copy = pltpu.make_async_copy(ids_hbm, ids_v, sm_sem.at[2])
    ids_copy.start()
    nodes_copy = pltpu.make_async_copy(nodes_hbm, nodes, sm_sem.at[3])
    nodes_copy.start()

    def w_copy(k):
        g = lax.rem(me // GROUPS + k, GROUPS)
        return pltpu.make_async_copy(
            w_hbm.at[:, pl.ds(pl.multiple_of(g * WCOL, 128), WCOL)], w_v.at[k], w_sem.at[k]
        )

    @pl.loop(0, GROUPS)
    def _(k):
        w_copy(k).start()

    wo_copy = pltpu.make_async_copy(wo_hbm, wo_v, w_sem.at[GROUPS])
    def kv_copy(c, d):
        peer = lax.rem(me + d, SEQ)
        return pltpu.make_async_remote_copy(
            src_ref=kvs[c].at[peer],
            dst_ref=kvc[c].at[pl.ds(OWN * me, OWN)],
            send_sem=kv_ss.at[c, d],
            recv_sem=kv_rs.at[c, d],
            device_id={"seq": peer},
            device_id_type=MESH,
        )

    def kv_own(c):
        return pltpu.make_async_copy(kvs[c].at[me], kvc[c].at[pl.ds(OWN * me, OWN)], own_sem.at[c])

    def q_copy(i, d):
        peer = lax.rem(me + d, SEQ)
        return pltpu.make_async_remote_copy(
            src_ref=qs.at[peer, i],
            dst_ref=qr.at[i, me],
            send_sem=q_ss.at[i, d],
            recv_sem=q_rs.at[i, d],
            device_id={"seq": peer},
            device_id_type=MESH,
        )

    def q_own(i):
        return pltpu.make_async_copy(qs.at[me, i], qr.at[i, me], own_sem.at[CH + i])

    def list_copy(d):
        peer = lax.rem(mc + d, CL)
        return pltpu.make_async_remote_copy(
            src_ref=lsend.at[peer],
            dst_ref=lrecv.at[CL - d],
            send_sem=l_ss.at[d],
            recv_sem=l_rs.at[d],
            device_id={"cluster": peer},
            device_id_type=MESH,
        )

    def z_copy(c, d):
        return pltpu.make_async_remote_copy(
            src_ref=snd[c].at[d],
            dst_ref=far[c].at[pl.ds(REQ * mc, REQ)],
            send_sem=z_ss.at[c, d],
            recv_sem=z_rs.at[c, d],
            device_id={"cluster": lax.rem(mc + d, CL)},
            device_id_type=MESH,
        )

    def ret_copy(i, peer, d):
        return pltpu.make_async_remote_copy(
            src_ref=outs.at[i, peer],
            dst_ref=ret.at[i, me],
            send_sem=r_ss.at[i, d],
            recv_sem=r_rs.at[i, d],
            device_id={"seq": peer},
            device_id_type=MESH,
        )

    def ret_own(i):
        return pltpu.make_async_copy(outs.at[i, me], ret.at[i, me], own_sem.at[CH + 2 + i])

    def start(own, copy):
        own.start()

        @pl.loop(1, SEQ)
        def _(d):
            copy(d).start()

    def start_after(done, own, copy):
        own.start()

        @pl.loop(1, SEQ)
        def _(d):
            done(d).wait_send()
            copy(d).start()

    def landed(own, copy):
        own.wait()

        @pl.loop(1, SEQ)
        def _(d):
            copy(d).wait_recv()

    def kv(c):
        return functools.partial(kv_copy, c)

    def qq(i):
        return functools.partial(q_copy, i)

    def pack(c):
        @pl.loop(1, CL)
        def _(d):
            for r in range(REQ):
                snd[c][d, r] = kvc[c][lsm[d, 0, r] & (QB - 1)]
            z_copy(c, d).start()

    turn[...] = jnp.zeros((128, 128), F32)
    ids_copy.wait()
    turn[:KVB, :QB] = ids_v[...].astype(F32)
    ids_t = jnp.transpose(turn[...])
    lane = lax.broadcasted_iota(jnp.int32, (QB, CL * QB), 1).astype(F32)
    hits = [ids_t[:QB, NEAR + j : NEAR + j + 1] == lane for j in range(REMOTE)]
    named = jnp.where(hits[0] | hits[1] | hits[2] | hits[3], 1.0, 0.0)
    present = jnp.max(named, axis=0, keepdims=True)
    present = jnp.broadcast_to(present, (8, CL * QB))
    lane8 = lax.broadcasted_iota(jnp.int32, (8, CL * QB), 1)
    inner = lane8 % QB
    rank = present
    step = 1
    while step < QB:
        rank = rank + jnp.where(inner >= step, pltpu.roll(rank, step, 1), 0.0)
        step *= 2
    rank = rank - present
    slot = lax.broadcasted_iota(jnp.int32, (REQ, CL * QB), 0).astype(F32)
    wanted = jnp.where((slot == rank[:1]) & (present[:1] > 0.5), 1.0, 0.0).astype(BF16)
    sub8 = lax.broadcasted_iota(jnp.int32, (CL, CL * QB), 0)
    worth = jnp.where(lane8 // QB == sub8, inner, 0).astype(F32).astype(BF16)
    wanted = jnp.concatenate([wanted, jnp.zeros((128 - REQ, CL * QB), BF16)], axis=0)
    lists = lax.dot_general(
        worth, wanted, (((1,), (1,)), ((), ())), preferred_element_type=F32
    ).astype(jnp.int32)
    for p in range(CL):
        lsend[p] = lists[p : p + 1]
    place = rank + (lane8 // QB * REQ).astype(F32)
    lane_q = lax.broadcasted_iota(jnp.int32, (QB, 128), 1)
    table = jnp.zeros((QB, 128), F32)
    for j in range(REMOTE):
        at = jnp.sum(jnp.where(hits[j], place[:1], 0.0), axis=1, keepdims=True)
        table = jnp.where(lane_q == j, at, table)
    far_v[...] = table.astype(jnp.int32)
    far_copy = pltpu.make_async_copy(far_v, far_s, sm_sem.at[1])
    far_copy.start()

    def project(k, x):
        p = jnp.dot(x, w_v[k], preferred_element_type=F32)
        return [[p[:, 384 * n + 128 * e : 384 * n + 128 * e + 128] for e in range(3)] for n in range(2)]

    def group(k):
        return lax.rem(me // GROUPS + k, GROUPS)

    def send_group(c, k):
        @pl.loop(0, HEADS // GROUPS)
        def _(h):
            d = lax.rem(group(k) * (HEADS // GROUPS) + h + SEQ - me, SEQ)

            @pl.when(d > 0)
            def _():
                kv_copy(c, d).start()

    nodes_copy.wait()
    x0 = jnp.concatenate([nodes[b * BLK : b * BLK + ROWS[0]] for b in range(OWN)], axis=0)

    @pl.loop(0, GROUPS)
    def _(k):
        w_copy(k).wait()
        low = low_lanes((OWN * ROWS[0], 128))
        for n, (t0, t1, t2) in enumerate(project(k, x0)):
            h0 = 4 * group(k) + 2 * n
            kv0 = jnp.where(low, swap_halves(t0), swap_halves(t1))
            kvs[0][h0] = kv0.astype(BF16).reshape(OWN, ROWS[0], 128)
            kvs[0][h0 + 1] = t2.astype(BF16).reshape(OWN, ROWS[0], 128)

        @pl.when(k == 0)
        def _():
            pl.semaphore_wait(barrier, SEQ + CL - 2)

            @pl.loop(1, CL)
            def _(d):
                list_copy(d).start()

        send_group(0, k)

    kv_own(0).start()
    wo_copy.start()

    @pl.loop(0, GROUPS)
    def _(k):
        @pl.when(k == GROUPS // 2)
        def _():
            @pl.loop(1, CL)
            def _(d):
                list_copy(d).wait()

            sm_copy = pltpu.make_async_copy(
                lrecv.at[pl.ds(1, CL - 1)], lsm.at[pl.ds(1, CL - 1)], sm_sem.at[0]
            )
            sm_copy.start()
            sm_copy.wait()


            landed(kv_own(0), kv(0))
            pack(0)

        low = low_lanes((OWN * BLK, 128))
        half = OWN * BLK // 2
        scale = HD**-0.5
        for n, (t0, t1, t2) in enumerate(project(k, nodes[...])):
            r0, r1 = swap_halves(t0), swap_halves(t1)
            h0 = 4 * group(k) + 2 * n
            kv0 = jnp.where(low, r0, r1).astype(BF16).reshape(OWN, BLK, 128)
            kv1 = t2.astype(BF16).reshape(OWN, BLK, 128)
            for c in range(1, CH):
                kvs[c][h0] = kv0[:, FIRST[c] : FIRST[c] + ROWS[c]]
                kvs[c][h0 + 1] = kv1[:, FIRST[c] : FIRST[c] + ROWS[c]]
            q0 = jnp.where(low[:half], t0[:half], r0[half:]) * scale
            q1 = jnp.where(low[:half], r1[:half], t1[half:]) * scale
            qs[h0] = q0.astype(BF16).reshape(2, BLK, 128)
            qs[h0 + 1] = q1.astype(BF16).reshape(2, BLK, 128)
        send_group(1, k)

    kv_own(1).start()
    start_after(kv(1), kv_own(2), kv(2))
    for c in range(1, CH):
        landed(kv_own(c), kv(c))
        pack(c)
        if c + 2 < CH:
            start_after(kv(c + 1), kv_own(c + 2), kv(c + 2))
        elif c + 2 == CH:
            start_after(kv(c + 1), q_own(0), qq(0))
    start_after(qq(0), q_own(1), qq(1))

    def block_of(bufs, b):
        return [bufs[c][b] for c in range(CH)]

    def pair_of(bufs, b0, b1):
        return jnp.concatenate(block_of(bufs, b0) + block_of(bufs, b1), axis=0)

    def near_pair(qb, j):
        return pair_of(kvc, ids_s[j, qb] & (QB - 1), ids_s[j + 1, qb] & (QB - 1))

    def far_pair(qb, j):
        last = CL * REQ - 1
        return pair_of(far, far_s[qb, j] & last, far_s[qb, j + 1] & last)

    def score(q, kv):
        return lax.dot_general(q, kv, (((1,), (1,)), ((), ())), preferred_element_type=F32)

    def weigh(s, m, kv):
        p = jnp.exp(s - m).astype(BF16)
        v1 = jnp.where(low_lanes(kv.shape), jnp.ones_like(kv), kv)
        return jnp.dot(p, v1, preferred_element_type=F32)

    def queries(i, s):
        qp = qr[i, s]
        low = low_lanes(qp.shape)
        left = jnp.where(low, qp, jnp.zeros_like(qp))
        right = jnp.where(low, swap_halves(qp.astype(F32)), 0.0).astype(BF16)
        return left, right

    def items_of(i, first, count):
        items = []
        for u in range(count // 2):
            s = lax.rem(me + first + u, SEQ)
            for half, q in enumerate(queries(i, s)):
                items.append((s, half, q, s * OWN + i + 2 * half))
        return items

    def near(i):
        @pl.loop(0, 2 * SEQ // WIDE)
        def _(t):
            items = items_of(i, t * (WIDE // 2), WIDE)
            tops = [None] * WIDE
            for jj in range(NEAR // 2):
                for g, (s, half, q, qb) in enumerate(items):
                    sco = score(q, near_pair(qb, 2 * jj))
                    sc[g, jj] = sco
                    top = jnp.maximum(sco[:, :BLK], sco[:, BLK:])
                    tops[g] = top if jj == 0 else jnp.maximum(tops[g], top)
            tops = [jnp.max(top, axis=1, keepdims=True) for top in tops]
            accs = [None] * WIDE
            for jj in range(NEAR // 2):
                for g, (s, half, q, qb) in enumerate(items):
                    a = weigh(sc[g, jj], tops[g], near_pair(qb, 2 * jj))
                    accs[g] = a if jj == 0 else accs[g] + a
            for g, (s, half, q, qb) in enumerate(items):
                acc_v[i, s, half] = accs[g]
                top_v[i, s, half] = jnp.broadcast_to(tops[g], (BLK, 128))

    def distant(i):
        @pl.loop(0, 2 * SEQ // SIDE)
        def _(t):
            items = items_of(i, t * (SIDE // 2), SIDE)
            pairs = [[far_pair(qb, 2 * jj) for jj in range(REMOTE // 2)] for _, _, _, qb in items]
            scores, tops, accs = [], [], []
            for g, (s, half, q, qb) in enumerate(items):
                pieces = []
                for jj in range(REMOTE // 2):
                    sco = score(q, pairs[g][jj])
                    for part in range(2):
                        piece = sco[:, part * BLK : (part + 1) * BLK]
                        slot = NEAR + 2 * jj + part
                        if slot >= LEAST:
                            piece = jnp.where(slot < cnt_s[qb], piece, -1e30)
                        pieces.append(piece)
                scores.append(pieces)
            for g, (s, half, q, qb) in enumerate(items):
                m = top_v[i, s, half]
                for piece in scores[g]:
                    m = jnp.maximum(m, piece)
                tops.append(jnp.max(m, axis=1, keepdims=True))
            for g, (s, half, q, qb) in enumerate(items):
                acc = acc_v[i, s, half] * jnp.exp(top_v[i, s, half] - tops[g])
                for jj in range(REMOTE // 2):
                    both = jnp.concatenate(scores[g][2 * jj : 2 * jj + 2], axis=1)
                    acc = acc + weigh(both, tops[g], pairs[g][jj])
                accs.append(acc)
            low = low_lanes((BLK, 128))
            for u in range(SIDE // 2):
                s = items[2 * u][0]
                left, right = accs[2 * u : 2 * u + 2]
                lsw, rsw = swap_halves(left), swap_halves(right)
                value = jnp.where(low, lsw, right)
                total = jnp.where(low, left, rsw)
                outs[i, s] = (value / total).astype(BF16)

            for u in range(SIDE // 2):
                d = t * (SIDE // 2) + u

                @pl.when(d > 0)
                def _(d=d):
                    ret_copy(i, lax.rem(me + d, SEQ), d).start()

    landed(q_own(0), qq(0))
    near(0)
    landed(q_own(1), qq(1))
    near(1)

    for c in range(CH):

        @pl.loop(1, CL)
        def _(d, c=c):
            z_copy(c, d).wait()

    far_copy.wait()
    for i in range(2):
        distant(i)
        ret_own(i).start()

    @pl.loop(1, SEQ)
    def _(d):
        q_copy(1, d).wait_send()
        kv_copy(0, d).wait_send()

    wo_copy.wait()
    for i in range(2):
        ret_own(i).wait()

        @pl.loop(1, SEQ)
        def _(d, i=i):
            ret_copy(i, lax.rem(me + d, SEQ), d).wait()

        for g in range(HEADS // 2):
            a = ret[i, 2 * g].astype(F32)
            b = ret[i, 2 * g + 1].astype(F32)
            low = low_lanes(a.shape)
            col = slice(g * 128, (g + 1) * 128)
            att[:BLK, col] = jnp.where(low, a, swap_halves(b)).astype(BF16)
            att[BLK:, col] = jnp.where(low, swap_halves(a), b).astype(BF16)
        out = jnp.dot(att[...], wo_v[...], preferred_element_type=F32).astype(BF16)
        o_ref[i] = out[:BLK]
        o_ref[2 + i] = out[BLK:]


def write_out(x_ref, o_ref, sem):
    copies = [pltpu.make_async_copy(x_ref.at[b], o_ref.at[b], sem.at[b]) for b in range(OWN)]
    for copy in copies:
        copy.start()
    for copy in copies:
        copy.wait()


def on_device(nodes, w_qkv, w_out, kv_ids, counts):
    vm = pl.BlockSpec(memory_space=pltpu.VMEM)
    sm = pl.BlockSpec(memory_space=pltpu.SMEM)
    hbm = pl.BlockSpec(memory_space=pl.ANY)
    dma = pltpu.SemaphoreType.DMA
    out = pl.pallas_call(
        body,
        out_shape=pltpu.VMEM((OWN, BLK, D), BF16),
        in_specs=[sm, sm, hbm, hbm, hbm, hbm],
        out_specs=vm,
        scratch_shapes=[
            *[pltpu.VMEM((HEADS, OWN, r, 128), BF16) for r in ROWS],
            *[pltpu.VMEM((QB, r, 128), BF16) for r in ROWS],
            *[pltpu.VMEM((CL, REQ, r, 128), BF16) for r in ROWS],
            *[pltpu.VMEM((CL * REQ, r, 128), BF16) for r in ROWS],
            pltpu.VMEM((GROUPS, D, WCOL), BF16),
            pltpu.VMEM((D, D), BF16),
            pltpu.VMEM((HEADS, 2, BLK, 128), BF16),
            pltpu.VMEM((2, SEQ, BLK, 128), BF16),
            pltpu.VMEM((CL, 1, 128), jnp.int32),
            pltpu.VMEM((CL, 1, 128), jnp.int32),
            pltpu.SMEM((CL, 1, 128), jnp.int32),
            pltpu.VMEM((QB, 128), jnp.int32),
            pltpu.SMEM((QB, 128), jnp.int32),
            pltpu.VMEM((WIDE, NEAR // 2, BLK, 2 * BLK), F32),
            pltpu.VMEM((2, SEQ, 2, BLK, 128), F32),
            pltpu.VMEM((2, SEQ, 2, BLK, 128), F32),
            pltpu.VMEM((2, SEQ, BLK, 128), BF16),
            pltpu.VMEM((2, SEQ, BLK, 128), BF16),
            pltpu.VMEM((2 * BLK, D), BF16),
            pltpu.VMEM((128, 128), F32),
            pltpu.VMEM((OWN * BLK, D), BF16),
            pltpu.VMEM((KVB, QB), jnp.int32),
            dma((GROUPS + 1,)),
            dma((CL,)),
            dma((CL,)),
            dma((CH, SEQ)),
            dma((CH, SEQ)),
            dma((2, SEQ)),
            dma((2, SEQ)),
            dma((CH, CL)),
            dma((CH, CL)),
            dma((2, SEQ)),
            dma((2, SEQ)),
            dma((CH + 4,)),
            dma((4,)),
        ],
        compiler_params=pltpu.CompilerParams(
            collective_id=0, has_side_effects=True, vmem_limit_bytes=60 << 20
        ),
        name="sublayer",
    )(kv_ids.T, counts, nodes, kv_ids.T, w_qkv, w_out)
    return pl.pallas_call(
        write_out,
        out_shape=jax.ShapeDtypeStruct((OWN, BLK, D), BF16),
        in_specs=[vm],
        out_specs=hbm,
        scratch_shapes=[dma((OWN,))],
        compiler_params=pltpu.CompilerParams(vmem_limit_bytes=1 << 20),
        name="write_out",
    )(out).reshape(OWN * BLK, D)


def solution(mesh):
    placed = (P(("cluster", "seq"), None), P(), P(), P("cluster", None), P("cluster"))
    return jax.shard_map(
        on_device,
        mesh=mesh,
        in_specs=placed,
        out_specs=P(("cluster", "seq"), None),
        check_vma=False,
    )
```
